128 devices in a mesh: grp: 2 (over z_lo), wide: 64 (over z_hi, y, x, core).
Axes of the slice: x: 4, y: 4, z: 4 (z_hi: 2, z_lo: 2; z = z_hi * 2 + z_lo), core: 2. Of those that a mesh axis runs over, the one named last changes fastest.
Arguments:
- tile_values: bfloat16 [1024, 512, 512], P('wide', None, 'grp'), may hold values from -200 to 1000
- tile_rows: int32 [1024], P('wide'), may hold values from 0 to 255, as said below
- tile_cols: int32 [1024], P('wide'), may hold values from 0 to 511, as said below
- objective: float32 [512, 512], P('wide', 'grp'), may hold values from -40 to 42
- demand: float32 [256, 512], P('wide', 'grp'), may hold values from -40 to 42
- primal_step: float32 [], replicated, may hold values from 0.5 to 0.95
- dual_step: float32 [], replicated, may hold values from 0.5 to 0.95
Outputs:
- primal_iterate: float32 [512, 512], P('wide', 'grp')
- dual_iterate: float32 [256, 512], P('wide', 'grp')
The draws below stay inside these ranges and needn't reach their ends.
Inputs may be any that keep to these rules, and one draw needn't show every extreme that they name: `tile_rows`: every block row is named by at least one tile; tiles may repeat a block position, and then they add. `tile_cols`: the 16 tiles held by index w of wide all lie in block columns w * 8 to (w + 1) * 8 - 1, and each of these columns is named by at least one of them.
All inputs are finite; a program needn't handle non-finite values.
Results may differ from the reference program's by a relative error of at most 0.0003.
Values may be sent and summed in bfloat16 or wider, within the bound.
A program may use at most 64 MiB of HBM per device.

```python
import jax
import jax.numpy as jnp
from jax import lax

BSZ = 512
BLOCKS_W = 16
CBW = 8
PASSES = 2
ITERS = 2
BR = 256
BC = 512
NBLK = 1024
N_WIDE = 64


def draw_tile_values(key, part):
    keys = jax.random.split(key, 3)
    base = jax.random.uniform(keys[0], (NBLK, BSZ, BSZ), jnp.float32, -1.0, 2.0)
    row_scale = 10.0 ** jax.random.uniform(keys[1], (NBLK, BSZ, 1), jnp.float32)
    col_scale = 10.0 ** jax.random.uniform(keys[2], (NBLK, 1, BSZ), jnp.float32)
    return (base * row_scale * col_scale).astype(jnp.bfloat16)


def draw_tile_rows(key, part):
    keys = jax.random.split(key, 2)
    extra = jax.random.randint(keys[0], (NBLK - BR,), 0, BR, jnp.int32)
    listed = jnp.concatenate([jnp.arange(BR, dtype=jnp.int32), extra])
    return jax.random.permutation(keys[1], listed).astype(jnp.int32)


def draw_tile_cols(key, part):
    groups = NBLK // BLOCKS_W

    def one_group(index):
        keys = jax.random.split(jax.random.fold_in(key, index), 2)
        extra = jax.random.randint(keys[0], (BLOCKS_W - CBW,), 0, CBW, jnp.int32)
        listed = jnp.concatenate([jnp.arange(CBW, dtype=jnp.int32), extra])
        return jax.random.permutation(keys[1], listed) + index * CBW
    return jax.vmap(one_group)(jnp.arange(groups, dtype=jnp.int32)).reshape(NBLK).astype(jnp.int32)


def ramped(key, count):
    ramp = (jnp.arange(count, dtype=jnp.float32) / count)[:, None]
    noise = jax.random.truncated_normal(key, -4.0, 4.0, (count, BSZ), jnp.float32)
    return noise * 10.0 ** ramp


def draw_objective(key, part):
    return ramped(jax.random.fold_in(key, 11), BC)


def draw_demand(key, part):
    return ramped(jax.random.fold_in(key, 23), BR)


def setup_inputs(seed: int = 0) -> dict:
    streams_of = jax.random.split(jax.random.key(seed), 8)
    tile_values = draw_tile_values(jax.random.fold_in(streams_of[7], 71), 0)
    tile_rows = draw_tile_rows(jax.random.fold_in(streams_of[7], 71), 0)
    tile_cols = draw_tile_cols(jax.random.fold_in(streams_of[7], 71), 0)
    objective = draw_objective(jax.random.fold_in(streams_of[7], 71), 0)
    demand = draw_demand(jax.random.fold_in(streams_of[7], 71), 0)
    primal_step = jnp.clip(jax.random.uniform(streams_of[5], (), jnp.float32, 0.5, 0.95), 0.5, 0.95)
    dual_step = jnp.clip(jax.random.uniform(streams_of[6], (), jnp.float32, 0.5, 0.95), 0.5, 0.95)
    return dict(tile_values=tile_values, tile_rows=tile_rows, tile_cols=tile_cols, objective=objective, demand=demand, primal_step=primal_step, dual_step=dual_step)


HIGHEST = lax.Precision.HIGHEST
EPSILON = 1e-06

def rounded(vector):
    return lax.optimization_barrier(vector.astype(jnp.bfloat16)).astype(jnp.float32)

def blockwise(tile_values, vectors, magnitude, transpose):

    def single(operands):
        matrix, vector = operands
        matrix = matrix.astype(jnp.float32)
        if magnitude:
            matrix = jnp.abs(matrix)
        if transpose:
            return jnp.einsum('kij,ki->kj', matrix, vector, precision=HIGHEST)
        return jnp.einsum('kij,kj->ki', matrix, vector, precision=HIGHEST)
    grouped = (tile_values.reshape(N_WIDE, BLOCKS_W, BSZ, BSZ), vectors.reshape(N_WIDE, BLOCKS_W, BSZ))
    return lax.map(single, grouped).reshape(N_WIDE * BLOCKS_W, BSZ)

def reference(tile_values, tile_rows, tile_cols, objective, demand, primal_step, dual_step):
    row_count = demand.shape[0]
    col_count = objective.shape[0]
    row_factor = jnp.ones((row_count, BSZ), jnp.float32)
    col_factor = jnp.ones((col_count, BSZ), jnp.float32)
    for repeat_index in range(PASSES):
        row_sum = jax.ops.segment_sum(blockwise(tile_values, rounded(col_factor)[tile_cols], True, False), tile_rows, num_segments=row_count)
        col_sum = jax.ops.segment_sum(blockwise(tile_values, rounded(row_factor)[tile_rows], True, True), tile_cols, num_segments=col_count)
        row_factor, col_factor = (row_factor / jnp.sqrt(row_factor * row_sum + EPSILON), col_factor / jnp.sqrt(col_factor * col_sum + EPSILON))

    def scale_group(operands):
        matrix, left, right = operands
        return (left[:, :, None] * matrix.astype(jnp.float32) * right[:, None, :]).astype(jnp.bfloat16)
    scaled = lax.map(scale_group, (tile_values.reshape(N_WIDE, BLOCKS_W, BSZ, BSZ), row_factor[tile_rows].reshape(N_WIDE, BLOCKS_W, BSZ), col_factor[tile_cols].reshape(N_WIDE, BLOCKS_W, BSZ))).reshape(N_WIDE * BLOCKS_W, BSZ, BSZ)
    all_ones = jnp.ones((N_WIDE * BLOCKS_W, BSZ), jnp.float32)
    row_abs = jax.ops.segment_sum(blockwise(scaled, all_ones, True, False), tile_rows, num_segments=row_count)
    col_abs = jax.ops.segment_sum(blockwise(scaled, all_ones, True, True), tile_cols, num_segments=col_count)
    primal_rate = primal_step / (col_abs + EPSILON)
    dual_rate = dual_step / (row_abs + EPSILON)
    cost_scaled = col_factor * objective
    demand_scaled = row_factor * demand
    cost_hat = cost_scaled / jnp.sqrt(jnp.sum(cost_scaled * cost_scaled) / (col_count * BSZ) + EPSILON)
    demand_hat = demand_scaled / jnp.sqrt(jnp.sum(demand_scaled * demand_scaled) / (row_count * BSZ) + EPSILON)
    primal = jnp.zeros((col_count, BSZ), jnp.float32)
    dual = jnp.zeros((row_count, BSZ), jnp.float32)
    for iteration in range(ITERS):
        pulled = jax.ops.segment_sum(blockwise(scaled, rounded(dual)[tile_rows], False, True), tile_cols, num_segments=col_count)
        primal_next = jnp.maximum(primal - primal_rate * (cost_hat - pulled), 0.0)
        pushed = jax.ops.segment_sum(blockwise(scaled, rounded(2.0 * primal_next - primal)[tile_cols], False, False), tile_rows, num_segments=row_count)
        dual = dual + dual_rate * (demand_hat - pushed)
        primal = primal_next
    return (primal, dual)
```

```python
import functools

import jax
import jax.numpy as jnp
from jax import lax
from jax.experimental import pallas as pl
from jax.experimental.pallas import tpu as pltpu
from jax.sharding import Mesh
from jax.sharding import PartitionSpec as P

AXES = ("grp", "zh", "y", "x", "core")
WIDE = AXES[1:]
EPSILON = 1e-06
MESH = pl.DeviceIdType.MESH
F32 = jnp.float32
BF16 = jnp.bfloat16
TILES = 16
CHUNK = 4

(E0, A1Q0, A1Q1, B1, B2, A2, SA, SB, A3Q0, A3Q1, B3, B4, A4, A5, B5) = range(15)
STAGES = 15


def iota(shape, dim):
    return lax.broadcasted_iota(jnp.int32, shape, dim)


def one_hot(condition):
    return jnp.where(condition, 1.0, 0.0).astype(BF16)


def split(value):
    high = value.astype(BF16)
    return high, (value - high.astype(F32)).astype(BF16)


def wait_bytes(ref, sem):
    pltpu.make_async_copy(ref, ref, sem).wait()


def dot(left, right):
    return lax.dot_general(left, right, (((1,), (0,)), ((), ())), preferred_element_type=F32)


def dot_nt(left, right):
    return lax.dot_general(left, right, (((1,), (1,)), ((), ())), preferred_element_type=F32)


def kernel(
    tile_rows,
    tile_cols,
    primal_step,
    dual_step,
    tiles_hbm,
    objective,
    demand,
    primal_out,
    dual_out,
    tiles,
    names,
    names_in,
    row_parts,
    buf_a1,
    buf_a3,
    buf_a5,
    send_b1,
    recv_b1,
    send_b3,
    recv_b3,
    send_b5,
    recv_b5,
    pay2,
    rows2,
    sel2,
    recv_a2,
    pay4,
    rows4,
    sel4,
    recv_a4,
    picked,
    hot1,
    hot2,
    hot4,
    hot5,
    scal,
    scal_a,
    scal_b_out,
    scal_b,
    demand8,
    pushed4,
    tile_sem,
    send_sem,
    recv_sem,
):
    g, zh, y, x, c = (lax.axis_index(axis) for axis in AXES)
    slot_me = (zh * 4 + y) * 2 + c

    def x_device(step):
        return (g, zh, y, lax.rem(x + step, 4), c)

    def plane(step):
        og, oc, oz, oy = (step & 1, (step >> 1) & 1, (step >> 2) & 1, step >> 3)
        return (
            lax.rem(g + og, 2),
            lax.rem(zh + oz, 2),
            lax.rem(y + oy, 4),
            lax.rem(c + oc, 2),
        )

    def send(src, dst, stage, device):
        pltpu.make_async_remote_copy(
            src_ref=src,
            dst_ref=dst,
            send_sem=send_sem.at[stage],
            recv_sem=recv_sem.at[stage],
            device_id=device,
            device_id_type=MESH,
        ).start()

    barrier = pltpu.get_barrier_semaphore()
    for step in range(1, 4):
        pl.semaphore_signal(barrier, inc=1, device_id=x_device(step), device_id_type=MESH)
    for step in range(1, 32):
        pg, pz, py, pc = plane(step)
        pl.semaphore_signal(barrier, inc=1, device_id=(pg, pz, py, x, pc), device_id_type=MESH)

    for chunk in range(TILES // CHUNK):
        part = pl.ds(chunk * CHUNK, CHUNK)
        pltpu.make_async_copy(tiles_hbm.at[part], tiles.at[part], tile_sem.at[chunk]).start()

    sub = iota((16, 128), 0)
    lane = iota((8, 128), 1)
    down = jnp.zeros((16, 128), jnp.int32)
    along = jnp.zeros((8, 128), jnp.int32)
    for k in range(TILES):
        down = jnp.where(sub == k, tile_rows[k], down)
        along = jnp.where((lane & 15) == k, tile_rows[k], along)
    names[0:16, :] = down
    names[16:24, :] = along
    demand8[0:4, :] = demand[...]
    demand8[4:8, :] = demand[...]

    ones_row = jnp.ones((16, 256), BF16)
    ones_col = jnp.ones((16, CHUNK * 512), BF16)
    eight = iota((8, 256), 0)

    def chunk_of(first):
        return tiles[pl.ds(first, CHUNK)].reshape(CHUNK * 512, 256)

    col_total = jnp.zeros((8, 256), F32)
    for chunk in range(TILES // CHUNK):
        part = pl.ds(chunk * CHUNK, CHUNK)
        pltpu.make_async_copy(tiles_hbm.at[part], tiles.at[part], tile_sem.at[chunk]).wait()
        block = jnp.abs(chunk_of(chunk * CHUNK))
        sums = dot_nt(ones_row, block)
        for j in range(CHUNK):
            k = chunk * CHUNK + j
            row_parts[k : k + 1, :] = sums[0:1, j * 512 : (j + 1) * 512]
            column = dot(ones_col[:, :512], block[j * 512 : (j + 1) * 512])
            col_total += jnp.where(eight == tile_cols[k], column[0:8], 0.0)

    pl.semaphore_wait(barrier, 34)

    def to_x(buf, rows, stage):
        for step in range(1, 4):
            send(buf.at[0, rows], buf.at[step, rows], stage, x_device(step))

    def to_plane(src, width, dst, stage):
        for step in range(31, 0, -1):
            pg, pz, py, pc = plane(step)
            target = (pz * 4 + py) * 2 + pc
            lanes = pl.ds(pl.multiple_of(pg * width, width), width)
            send(src.at[target, :, lanes], dst.at[step - 1], stage, (pg, pz, py, x, pc))

    def share(buf, base, stage):
        high, low = split(row_parts[...])
        buf[0, base : base + 16, :] = high
        buf[0, base + 16 : base + 32, :] = low
        to_x(buf, pl.ds(base, 32), stage)

    for step in range(1, 4):
        send(names, names_in.at[step - 1], E0, x_device(step))
    share(buf_a1, 0, A1Q0)

    row16 = iota((16, 512), 0) & 7

    def row_products(left, magnitude):
        def body(step, carry):
            first = step * CHUNK
            block = chunk_of(first)
            if magnitude:
                block = jnp.abs(block)
            sums = dot_nt(left, block)
            for j in range(CHUNK):
                mine = jnp.where(
                    row16 == tile_cols[first + j], sums[:, j * 512 : (j + 1) * 512], 0.0
                )
                row_parts[pl.ds(first + j, 1), :] = jnp.sum(mine, axis=0, keepdims=True)
            return carry

        lax.fori_loop(0, TILES // CHUNK, body, 0)

    eight_wide = iota((8, 512), 0)

    def column_products(kinds, magnitude):
        height = 16 * ((kinds + 1) // 2)

        def body(step, total):
            first = step * CHUNK
            lefts = []
            for j in range(CHUNK):
                k = first + j
                mine = eight_wide == tile_cols[k]
                pieces = [
                    jnp.where(mine, picked[pl.ds(kind * 16 + k, 1), :], 0.0)
                    for kind in range(kinds)
                ]
                while len(pieces) * 8 < height:
                    pieces.append(jnp.zeros((8, 512), F32))
                lefts.append(jnp.concatenate(pieces, axis=0).astype(BF16))
            block = chunk_of(first)
            if magnitude:
                block = jnp.abs(block)
            return total + dot(jnp.concatenate(lefts, axis=1), block)

        return lax.fori_loop(0, TILES // CHUNK, body, jnp.zeros((height, 256), F32))

    col_factor = 1.0 / jnp.sqrt(col_total + EPSILON)
    rounded = jnp.concatenate([col_factor, jnp.zeros_like(col_factor)], axis=0).astype(BF16)
    row_products(rounded, True)
    share(buf_a1, 32, A1Q1)

    wait_bytes(names_in, recv_sem.at[E0])
    lane_names = [names[16:17, :]] + [names_in[p, 16:17, :] for p in range(3)]
    down_names = [names[0:16, :]] + [names_in[p, 0:16, :] for p in range(3)]
    low_half = iota((1, 128), 1) < 64
    wide_names = jnp.concatenate(
        [
            jnp.where(low_half, lane_names[0], lane_names[1]),
            jnp.where(low_half, lane_names[2], lane_names[3]),
        ],
        axis=1,
    )
    m = iota((128, 256), 0)
    n = iota((128, 256), 1)

    def row_id(slot, index):
        return ((((slot >> 1) * 4 + x) * 2 + (slot & 1)) * 4) + index

    ids = row_id(m >> 3, m & 3)
    kind = (m >> 2) & 1
    hot1[...] = one_hot(jnp.logical_and(wide_names == ids, ((n >> 5) & 1) == kind))
    quarter = iota((1, 128), 1) >> 5
    narrow = lane_names[3]
    for p in range(3):
        narrow = jnp.where(quarter == p, lane_names[p], narrow)
    narrow = jnp.concatenate([narrow, narrow], axis=1)
    hot5[...] = one_hot(jnp.logical_and(narrow == ids, (n >> 7) == kind))
    n16 = iota((16, 256), 1)
    ids16 = row_id(n16 >> 4, n16 & 3)
    group = (n16 >> 2) & 3
    for p in range(4):
        named = jnp.concatenate([down_names[p], down_names[p]], axis=1) == ids16
        for q, place in enumerate((0, 1, 3)):
            at = p * 48 + q * 16
            hot2[at : at + 16, :] = one_hot(jnp.logical_and(named, group == place))
        for q in range(2):
            at = p * 32 + q * 16
            hot4[at : at + 16, :] = one_hot(jnp.logical_and(named, group == q))

    def to_owner(buf, send_b, recv_b, stage):
        dense = dot(hot1[...], buf[...].reshape(256, 512))
        send_b[...] = dense.reshape(16, 8, 512)
        to_plane(send_b, 256, recv_b, stage)

    def own_total(send_b, recv_b, width, stage):
        mine = send_b[slot_me]
        mine = jnp.where(g == 0, mine[:, :width], mine[:, width:])
        wait_bytes(recv_b, recv_sem.at[stage])
        return mine + jnp.sum(recv_b[...], axis=0)

    def both(total):
        swapped = pltpu.roll(total, 4, 0)
        upper = eight < 4
        return jnp.where(upper, total, swapped), jnp.where(upper, swapped, total)

    wait_bytes(buf_a1.at[1:4, 0:32], recv_sem.at[A1Q0])
    wait_bytes(buf_a1.at[1:4, 32:64], recv_sem.at[A1Q1])
    to_owner(buf_a1, send_b1, recv_b1, B1)
    first_sum, second_sum = both(own_total(send_b1, recv_b1, 256, B1))
    row_first = 1.0 / jnp.sqrt(first_sum + EPSILON)
    row_factor = row_first / jnp.sqrt(row_first * second_sum + EPSILON)
    upper = eight < 4
    zeros8 = jnp.zeros((8, 256), F32)

    def to_holders(pay, rows, stage_b, hot, sel, recv, stage_a):
        kinds = sel.shape[1]
        lanes = pl.ds(pl.multiple_of(g * 256, 256), 256)
        for step in range(31, 0, -1):
            pg, pz, py, pc = plane(step)
            send(pay, rows.at[slot_me, :, lanes], stage_b, (pg, pz, py, x, pc))
        pltpu.make_async_copy(pay, rows.at[slot_me, :, lanes], recv_sem.at[stage_b]).start()
        wait_bytes(rows, recv_sem.at[stage_b])
        chosen = dot(hot[...], rows[...].reshape(256, 512)).astype(BF16)
        sel[...] = chosen.reshape(4, kinds, 512)
        for step in range(1, 4):
            send(sel.at[step], recv.at[step - 1], stage_a, x_device(4 - step))
        own = sel[0].astype(F32)
        wait_bytes(recv, recv_sem.at[stage_a])
        for p in range(3):
            own = own + recv[p].astype(F32)
        picked[0:kinds, :] = own

    high = row_factor.astype(BF16).astype(F32)
    pay2[...] = jnp.concatenate(
        [
            jnp.where(upper, row_first, row_factor),
            jnp.where(upper, 0.0, row_factor - high),
        ],
        axis=0,
    ).astype(BF16)
    to_holders(pay2, rows2, B2, hot2, sel2, recv_a2, A2)

    sums = column_products(3, True)
    col_next = col_factor / jnp.sqrt(col_factor * sums[0:8] + EPSILON)
    col_abs = col_next * (sums[8:16] + sums[16:24])
    primal_rate = primal_step[0] / (col_abs + EPSILON)
    cost_scaled = col_next * objective[...]
    demand_scaled = row_factor * demand8[...]

    def squares(value):
        return jnp.sum(jnp.sum(value * value, axis=0, keepdims=True), axis=1, keepdims=True)

    lanes1 = iota((1, 128), 1)
    scal[...] = jnp.where(
        lanes1 < 64, squares(cost_scaled), squares(jnp.where(upper, demand_scaled, 0.0))
    )
    for step in range(1, 4):
        send(scal, scal_a.at[step - 1], SA, x_device(step))

    def high_low(value):
        top = value.astype(BF16).astype(F32)
        return jnp.concatenate([top, value - top], axis=0).astype(BF16)

    row_products(high_low(col_next), True)
    share(buf_a3, 0, A3Q0)
    unit = jnp.maximum(-primal_rate * cost_scaled, 0.0)
    row_products(high_low(col_next * (2.0 * unit)), False)
    share(buf_a3, 32, A3Q1)

    wait_bytes(scal_a, recv_sem.at[SA])
    scal_b_out[...] = scal[...] + scal_a[0] + scal_a[1] + scal_a[2]
    for step in range(31, 0, -1):
        pg, pz, py, pc = plane(step)
        send(scal_b_out, scal_b.at[step - 1], SB, (pg, pz, py, x, pc))

    wait_bytes(buf_a3.at[1:4, 0:32], recv_sem.at[A3Q0])
    wait_bytes(buf_a3.at[1:4, 32:64], recv_sem.at[A3Q1])
    to_owner(buf_a3, send_b3, recv_b3, B3)
    wait_bytes(scal_b, recv_sem.at[SB])
    both_squares = scal_b_out[...] + jnp.sum(scal_b[...], axis=0)
    wide_count = 64
    cost_gain = 1.0 / jnp.sqrt(both_squares[:, 0:1] / (8 * wide_count * 512) + EPSILON)
    demand_gain = 1.0 / jnp.sqrt(both_squares[:, 64:65] / (4 * wide_count * 512) + EPSILON)
    primal = cost_gain * unit
    cost_hat = cost_scaled * cost_gain
    demand_hat = demand_scaled * demand_gain

    row_abs, pushed = both(own_total(send_b3, recv_b3, 256, B3))
    dual_rate = dual_step[0] / (row_factor * row_abs + EPSILON)
    dual = dual_rate * (demand_hat - row_factor * (pushed * cost_gain))
    weighted = row_factor * dual.astype(BF16).astype(F32)
    top = weighted.astype(BF16).astype(F32)
    pay4[...] = jnp.concatenate(
        [jnp.where(upper, weighted, weighted - top), zeros8], axis=0
    ).astype(BF16)
    to_holders(pay4, rows4, B4, hot4, sel4, recv_a4, A4)

    sums = column_products(2, False)
    pulled = col_next * (sums[0:8] + sums[8:16])
    primal_next = jnp.maximum(primal - primal_rate * (cost_hat - pulled), 0.0)
    primal_out[...] = primal_next
    bar = (2.0 * primal_next - primal).astype(BF16).astype(F32)
    row_products(high_low(col_next * bar), False)
    share(buf_a5, 0, A5)
    wait_bytes(buf_a5.at[1:4], recv_sem.at[A5])
    terms = buf_a5[...].reshape(128, 512)
    terms = jnp.concatenate(
        [
            jnp.concatenate([terms[:, 0:128], terms[:, 256:384]], axis=1),
            jnp.concatenate([terms[:, 128:256], terms[:, 384:512]], axis=1),
        ],
        axis=0,
    )
    send_b5[...] = dot(hot5[...], terms).reshape(16, 8, 256)
    to_plane(send_b5, 128, recv_b5, B5)
    total = own_total(send_b5, recv_b5, 128, B5)
    pushed4[:, 0:128] = total[0:4]
    pushed4[:, 128:256] = total[4:8]
    dual_out[...] = dual[0:4] + dual_rate[0:4] * (
        demand_hat[0:4] - row_factor[0:4] * pushed4[...]
    )

    wait_bytes(names_in, send_sem.at[E0])
    wait_bytes(buf_a1.at[1:4, 0:32], send_sem.at[A1Q0])
    wait_bytes(buf_a1.at[1:4, 32:64], send_sem.at[A1Q1])
    wait_bytes(recv_b1, send_sem.at[B1])
    for rows, pay, stage in ((recv_b1, pay2, B2), (recv_b3, pay4, B4)):
        wait_bytes(rows, send_sem.at[stage])
    wait_bytes(recv_a2, send_sem.at[A2])
    wait_bytes(scal_a, send_sem.at[SA])
    wait_bytes(scal_b, send_sem.at[SB])
    wait_bytes(buf_a3.at[1:4, 0:32], send_sem.at[A3Q0])
    wait_bytes(buf_a3.at[1:4, 32:64], send_sem.at[A3Q1])
    wait_bytes(recv_b3, send_sem.at[B3])
    wait_bytes(recv_a4, send_sem.at[A4])
    wait_bytes(buf_a5.at[1:4], send_sem.at[A5])
    wait_bytes(recv_b5, send_sem.at[B5])


def on_device(tile_values, tile_rows, tile_cols, objective, demand, primal_step, dual_step):
    wide_index = lax.axis_index(WIDE)
    vmem = pl.BlockSpec(memory_space=pltpu.VMEM)
    smem = pl.BlockSpec(memory_space=pltpu.SMEM)
    return pl.pallas_call(
        kernel,
        out_shape=(
            jax.ShapeDtypeStruct(objective.shape, F32),
            jax.ShapeDtypeStruct(demand.shape, F32),
        ),
        in_specs=[smem, smem, smem, smem, pl.BlockSpec(memory_space=pl.ANY), vmem, vmem],
        out_specs=(vmem, vmem),
        scratch_shapes=[
            pltpu.VMEM((TILES, 512, 256), BF16),
            pltpu.VMEM((24, 128), jnp.int32),
            pltpu.VMEM((3, 24, 128), jnp.int32),
            pltpu.VMEM((16, 512), F32),
            pltpu.VMEM((4, 64, 512), BF16),
            pltpu.VMEM((4, 64, 512), BF16),
            pltpu.VMEM((4, 32, 512), BF16),
            pltpu.VMEM((16, 8, 512), F32),
            pltpu.VMEM((31, 8, 256), F32),
            pltpu.VMEM((16, 8, 512), F32),
            pltpu.VMEM((31, 8, 256), F32),
            pltpu.VMEM((16, 8, 256), F32),
            pltpu.VMEM((31, 8, 128), F32),
            pltpu.VMEM((16, 256), BF16),
            pltpu.VMEM((16, 16, 512), BF16),
            pltpu.VMEM((4, 48, 512), BF16),
            pltpu.VMEM((3, 48, 512), BF16),
            pltpu.VMEM((16, 256), BF16),
            pltpu.VMEM((16, 16, 512), BF16),
            pltpu.VMEM((4, 32, 512), BF16),
            pltpu.VMEM((3, 32, 512), BF16),
            pltpu.VMEM((48, 512), F32),
            pltpu.VMEM((128, 256), BF16),
            pltpu.VMEM((192, 256), BF16),
            pltpu.VMEM((128, 256), BF16),
            pltpu.VMEM((128, 256), BF16),
            pltpu.VMEM((1, 128), F32),
            pltpu.VMEM((3, 1, 128), F32),
            pltpu.VMEM((1, 128), F32),
            pltpu.VMEM((31, 1, 128), F32),
            pltpu.VMEM((8, 256), F32),
            pltpu.VMEM((4, 256), F32),
            pltpu.SemaphoreType.DMA((TILES // CHUNK,)),
            pltpu.SemaphoreType.DMA((STAGES,)),
            pltpu.SemaphoreType.DMA((STAGES,)),
        ],
        compiler_params=pltpu.CompilerParams(collective_id=0, has_side_effects=True),
    )(
        tile_rows,
        tile_cols - wide_index * objective.shape[0],
        primal_step.reshape(1),
        dual_step.reshape(1),
        tile_values,
        objective,
        demand,
    )


def solution(mesh):
    devices = mesh.devices.reshape(mesh.shape["grp"], 2, 4, 4, 2)
    return jax.shard_map(
        on_device,
        mesh=Mesh(devices, AXES),
        in_specs=(P(WIDE, None, "grp"), P(WIDE), P(WIDE), P(WIDE, "grp"), P(WIDE, "grp"), P(), P()),
        out_specs=(P(WIDE, "grp"), P(WIDE, "grp")),
        check_vma=False,
    )
```

```python
import functools

import jax
import jax.numpy as jnp
from jax import lax
from jax.experimental import pallas as pl
from jax.experimental.pallas import tpu as pltpu
from jax.sharding import Mesh
from jax.sharding import PartitionSpec as P

AXES = ("grp", "zh", "y", "x", "core")
WIDE = AXES[1:]
EPSILON = 1e-06
MESH = pl.DeviceIdType.MESH
F32 = jnp.float32
BF16 = jnp.bfloat16
TILES = 16
CHUNK = 4
LOAD = 2

NAMES, SCAL_X, SCAL_PLANE = range(3)
UP_X, UP_PLANE, DOWN_PLANE, DOWN_X = 3, 8, 13, 15
STAGES = 17


def iota(shape, dim):
    return lax.broadcasted_iota(jnp.int32, shape, dim)


def one_hot(condition):
    return jnp.where(condition, 1.0, 0.0).astype(BF16)


def split(value):
    high = value.astype(BF16)
    return high, (value - high.astype(F32)).astype(BF16)


def wait_bytes(ref, sem):
    pltpu.make_async_copy(ref, ref, sem).wait()


def dot(left, right):
    return lax.dot_general(left, right, (((1,), (0,)), ((), ())), preferred_element_type=F32)


def dot_nt(left, right):
    return lax.dot_general(left, right, (((1,), (1,)), ((), ())), preferred_element_type=F32)


def kernel(
    tile_rows,
    tile_cols,
    primal_step,
    dual_step,
    tiles_hbm,
    objective,
    demand,
    primal_out,
    dual_out,
    tiles,
    flipped,
    names,
    names_in,
    row_parts,
    buf_a,
    send_b,
    recv_b,
    pay,
    rows,
    sel,
    recv_a,
    picked,
    hot_up,
    hot_down,
    scal,
    scal_x,
    scal_out,
    scal_in,
    demand8,
    tile_sem,
    send_sem,
    recv_sem,
):
    g, zh, y, x, c = (lax.axis_index(axis) for axis in AXES)
    slot_me = (zh * 4 + y) * 2 + c
    first_col = ((slot_me >> 1) * 4 + x) * 2 + c
    first_col = first_col * objective.shape[0]

    def x_device(step):
        return (g, zh, y, lax.rem(x + step, 4), c)

    def plane(step):
        og, oc, oz, oy = (step & 1, (step >> 1) & 1, (step >> 2) & 1, step >> 3)
        return (
            lax.rem(g + og, 2),
            lax.rem(zh + oz, 2),
            lax.rem(y + oy, 4),
            lax.rem(c + oc, 2),
        )

    def send(src, dst, stage, device):
        pltpu.make_async_remote_copy(
            src_ref=src,
            dst_ref=dst,
            send_sem=send_sem.at[stage],
            recv_sem=recv_sem.at[stage],
            device_id=device,
            device_id_type=MESH,
        ).start()

    barrier = pltpu.get_barrier_semaphore()
    for step in range(1, 4):
        pl.semaphore_signal(barrier, inc=1, device_id=x_device(step), device_id_type=MESH)
    for step in range(1, 32):
        pg, pz, py, pc = plane(step)
        pl.semaphore_signal(barrier, inc=1, device_id=(pg, pz, py, x, pc), device_id_type=MESH)

    def load(chunk):
        part = pl.ds(chunk * LOAD, LOAD)
        return pltpu.make_async_copy(tiles_hbm.at[part], tiles.at[part], tile_sem.at[chunk])

    for chunk in range(TILES // LOAD):
        load(chunk).start()

    sub = iota((16, 128), 0)
    lane = iota((8, 128), 1)
    down = jnp.zeros((16, 128), jnp.int32)
    along = jnp.zeros((8, 128), jnp.int32)
    for k in range(TILES):
        down = jnp.where(sub == k, tile_rows[k], down)
        along = jnp.where((lane & 15) == k, tile_rows[k], along)
    names[0:16, :] = down
    names[16:24, :] = along
    demand8[0:4, :] = demand[:, 0:128]
    demand8[4:8, :] = demand[:, 128:256]

    def column_of(k):
        return tile_cols[k] - first_col

    ones_row = jnp.ones((16, 256), BF16)
    eight = iota((8, 256), 0)
    col_total = jnp.zeros((8, 256), F32)
    for chunk in range(TILES // LOAD):
        load(chunk).wait()
        for k in range(chunk * LOAD, (chunk + 1) * LOAD):
            block = jnp.abs(tiles[k])
            row_parts[k : k + 1, :] = dot_nt(ones_row, block)[0:1]
            column = jnp.sum(block.astype(F32), axis=0, keepdims=True)
            col_total += jnp.where(eight == column_of(k), column, 0.0)

    def stage_up(q):
        high, low = split(row_parts[...])
        buf_a[q, 0, 0:16, :] = high
        buf_a[q, 0, 16:32, :] = low

    def send_up(q):
        for step in (2, 1, 3):
            send(buf_a.at[q, 0], buf_a.at[q, step], UP_X + q, x_device(step))

    row16 = iota((16, 512), 0) & 7

    def row_products(left, magnitude, turned=True, start=0, stop=TILES):
        def body(step, carry):
            for j in range(CHUNK):
                k = step * CHUNK + j
                block = flipped[k] if turned else tiles[k]
                if magnitude:
                    block = jnp.abs(block)
                sums = dot(left, block) if turned else dot_nt(left, block)
                mine = jnp.where(row16 == column_of(k), sums, 0.0)
                row_parts[pl.ds(k, 1), :] = jnp.sum(mine, axis=0, keepdims=True)
            return carry

        lax.fori_loop(start // CHUNK, stop // CHUNK, body, 0)

    eight_wide = iota((8, 512), 0)

    def column_products(magnitude):
        def body(step, total):
            lefts = []
            for j in range(CHUNK):
                k = step * CHUNK + j
                mine = eight_wide == column_of(k)
                pieces = [
                    jnp.where(mine, picked[pl.ds(kind * 16 + k, 1), :], 0.0) for kind in range(2)
                ]
                lefts.append(jnp.concatenate(pieces, axis=0).astype(BF16))
            block = tiles[pl.ds(step * CHUNK, CHUNK)].reshape(CHUNK * 512, 256)
            if magnitude:
                block = jnp.abs(block)
            return total + dot(jnp.concatenate(lefts, axis=1), block)

        return lax.fori_loop(0, TILES // CHUNK, body, jnp.zeros((16, 256), F32))

    def flip(start, stop):
        def body(step, carry):
            for j in range(2):
                k = step * 2 + j
                flipped[k] = tiles[k].T
            return carry

        lax.fori_loop(start // 2, stop // 2, body, 0)

    stage_up(0)
    col_factor = 1.0 / jnp.sqrt(col_total + EPSILON)
    rounded = jnp.concatenate([col_factor, jnp.zeros_like(col_factor)], axis=0).astype(BF16)
    row_products(rounded, True, False, 0, TILES // 2)
    pl.semaphore_wait(barrier, 34)
    for step in (2, 1, 3):
        send(names, names_in.at[step - 1], NAMES, x_device(step))
    send_up(0)
    row_products(rounded, True, False, TILES // 2, TILES)
    stage_up(1)
    send_up(1)

    flip(0, 4)
    wait_bytes(names_in, recv_sem.at[NAMES])
    lane_names = [names[16:17, :]] + [names_in[p, 16:17, :] for p in range(3)]
    down_names = [names[0:16, :]] + [names_in[p, 0:16, :] for p in range(3)]
    quarter = iota((1, 128), 1) >> 5
    narrow = lane_names[3]
    for p in range(3):
        narrow = jnp.where(quarter == p, lane_names[p], narrow)
    narrow = jnp.concatenate([narrow, narrow], axis=1)
    m = iota((128, 256), 0)
    n = iota((128, 256), 1)

    def row_id(slot, index):
        return ((((slot >> 1) * 4 + x) * 2 + (slot & 1)) * 4) + index

    hot_up[...] = one_hot(
        jnp.logical_and(narrow == row_id(m >> 3, m & 3), (n >> 7) == ((m >> 2) & 1))
    )
    n16 = iota((16, 256), 1)
    ids16 = row_id(n16 >> 4, n16 & 3)
    group = (n16 >> 2) & 3
    for p in range(4):
        named = jnp.concatenate([down_names[p], down_names[p]], axis=1) == ids16
        for half in range(2):
            for kind in range(2):
                at = p * 64 + half * 32 + kind * 16
                hot_down[at : at + 16, :] = one_hot(
                    jnp.logical_and(named, group == kind * 2 + half)
                )

    def to_owner(q):
        wait_bytes(buf_a.at[q, 1:4], recv_sem.at[UP_X + q])
        terms = buf_a[q].reshape(128, 512)
        terms = jnp.concatenate(
            [
                jnp.concatenate([terms[:, 0:128], terms[:, 256:384]], axis=1),
                jnp.concatenate([terms[:, 128:256], terms[:, 384:512]], axis=1),
            ],
            axis=0,
        )
        send_b[q] = dot(hot_up[...], terms).reshape(16, 8, 256)
        for step in range(31, 0, -1):
            pg, pz, py, pc = plane(step)
            target = (pz * 4 + py) * 2 + pc
            lanes = pl.ds(pl.multiple_of(pg * 128, 128), 128)
            send(
                send_b.at[q, target, :, lanes],
                recv_b.at[q, step - 1],
                UP_PLANE + q,
                (pg, pz, py, x, pc),
            )

    def own_total(q):
        mine = send_b[q, slot_me]
        mine = jnp.where(g == 0, mine[:, 0:128], mine[:, 128:256])
        wait_bytes(recv_b.at[q], recv_sem.at[UP_PLANE + q])
        return mine + jnp.sum(recv_b[q], axis=0)

    def to_holders(t, first, second, meanwhile):
        pay[t] = jnp.concatenate([first, second], axis=0).astype(BF16)
        for step in range(31, 0, -1):
            pg, pz, py, pc = plane(step)
            send(pay.at[t], rows.at[t, g, slot_me], DOWN_PLANE + t, (pg, pz, py, x, pc))
        pltpu.make_async_copy(
            pay.at[t], rows.at[t, g, slot_me], recv_sem.at[DOWN_PLANE + t]
        ).start()
        meanwhile()
        wait_bytes(rows.at[t], recv_sem.at[DOWN_PLANE + t])
        for half in range(2):
            chosen = dot(hot_down[...], rows[t, half].reshape(256, 128)).astype(BF16)
            for p in range(4):
                for quarter in range(2):
                    at = (half * 2 + quarter) * 128
                    begin = p * 64 + quarter * 32
                    sel[t, p, :, at : at + 128] = chosen[begin : begin + 32]
        for step in (2, 1, 3):
            send(sel.at[t, step], recv_a.at[t, step - 1], DOWN_X + t, x_device(4 - step))
        own = sel[t, 0].astype(F32)
        wait_bytes(recv_a.at[t], recv_sem.at[DOWN_X + t])
        for p in range(3):
            own = own + recv_a[t, p].astype(F32)
        picked[...] = own

    to_owner(0)
    to_owner(1)
    flip(4, 10)
    first_sum = own_total(0)
    second_sum = own_total(1)
    row_first = 1.0 / jnp.sqrt(first_sum + EPSILON)
    row_factor = row_first / jnp.sqrt(row_first * second_sum + EPSILON)
    to_holders(0, row_first, row_factor, lambda: flip(10, TILES))

    sums = column_products(True)
    col_next = col_factor / jnp.sqrt(col_factor * sums[0:8] + EPSILON)
    col_abs = col_next * sums[8:16]
    primal_rate = primal_step[0] / (col_abs + EPSILON)
    cost_scaled = col_next * objective[...]
    demand_scaled = row_factor * demand8[...]

    def squares(value):
        return jnp.sum(jnp.sum(value * value, axis=0, keepdims=True), axis=1, keepdims=True)

    scal[...] = jnp.where(iota((1, 128), 1) < 64, squares(cost_scaled), squares(demand_scaled))
    for step in (2, 1, 3):
        send(scal, scal_x.at[step - 1], SCAL_X, x_device(step))

    def high_low(value):
        top = value.astype(BF16).astype(F32)
        return jnp.concatenate([top, value - top], axis=0).astype(BF16)

    row_products(high_low(col_next), True)
    stage_up(2)
    send_up(2)
    unit = jnp.maximum(-primal_rate * cost_scaled, 0.0)
    row_products(high_low(col_next * (2.0 * unit)), False)
    stage_up(3)
    send_up(3)

    wait_bytes(scal_x, recv_sem.at[SCAL_X])
    scal_out[...] = scal[...] + scal_x[0] + scal_x[1] + scal_x[2]
    for step in range(31, 0, -1):
        pg, pz, py, pc = plane(step)
        send(scal_out, scal_in.at[step - 1], SCAL_PLANE, (pg, pz, py, x, pc))
    to_owner(2)
    to_owner(3)
    wait_bytes(scal_in, recv_sem.at[SCAL_PLANE])
    both_squares = scal_out[...] + jnp.sum(scal_in[...], axis=0)
    wide_count = 64
    cost_gain = 1.0 / jnp.sqrt(both_squares[:, 0:1] / (8 * wide_count * 512) + EPSILON)
    demand_gain = 1.0 / jnp.sqrt(both_squares[:, 64:65] / (4 * wide_count * 512) + EPSILON)
    primal = cost_gain * unit
    cost_hat = cost_scaled * cost_gain
    demand_hat = demand_scaled * demand_gain

    dual_rate = dual_step[0] / (row_factor * own_total(2) + EPSILON)
    dual = dual_rate * (demand_hat - row_factor * (own_total(3) * cost_gain))
    weighted = row_factor * dual.astype(BF16).astype(F32)
    top = weighted.astype(BF16).astype(F32)
    to_holders(1, top, weighted - top, lambda: None)

    sums = column_products(False)
    pulled = col_next * (sums[0:8] + sums[8:16])
    primal_next = jnp.maximum(primal - primal_rate * (cost_hat - pulled), 0.0)
    primal_out[...] = primal_next
    bar = (2.0 * primal_next - primal).astype(BF16).astype(F32)
    row_products(high_low(col_next * bar), False)
    stage_up(4)
    send_up(4)
    to_owner(4)
    dual_next = dual + dual_rate * (demand_hat - row_factor * own_total(4))
    dual_out[:, 0:128] = dual_next[0:4]
    dual_out[:, 128:256] = dual_next[4:8]

    wait_bytes(names_in, send_sem.at[NAMES])
    wait_bytes(scal_x, send_sem.at[SCAL_X])
    wait_bytes(scal_in, send_sem.at[SCAL_PLANE])
    for q in range(5):
        wait_bytes(buf_a.at[q, 1:4], send_sem.at[UP_X + q])
        wait_bytes(recv_b.at[q], send_sem.at[UP_PLANE + q])
    for t in range(2):
        wait_bytes(recv_b.at[t], send_sem.at[DOWN_PLANE + t])
        wait_bytes(recv_a.at[t], send_sem.at[DOWN_X + t])


def hand_over(primal, dual, primal_out, dual_out):
    primal_out[...] = primal[...]
    dual_out[...] = dual[...]


def on_device(tile_values, tile_rows, tile_cols, objective, demand, primal_step, dual_step):
    vmem = pl.BlockSpec(memory_space=pltpu.VMEM)
    smem = pl.BlockSpec(memory_space=pltpu.SMEM)
    shapes = (
        jax.ShapeDtypeStruct(objective.shape, F32),
        jax.ShapeDtypeStruct(demand.shape, F32),
    )
    results = pl.pallas_call(
        kernel,
        out_shape=shapes,
        in_specs=[smem, smem, smem, smem, pl.BlockSpec(memory_space=pl.ANY), vmem, vmem],
        out_specs=(vmem, vmem),
        scratch_shapes=[
            pltpu.VMEM((TILES, 512, 256), BF16),
            pltpu.VMEM((TILES, 256, 512), BF16),
            pltpu.VMEM((24, 128), jnp.int32),
            pltpu.VMEM((3, 24, 128), jnp.int32),
            pltpu.VMEM((16, 512), F32),
            pltpu.VMEM((5, 4, 32, 512), BF16),
            pltpu.VMEM((5, 16, 8, 256), F32),
            pltpu.VMEM((5, 31, 8, 128), F32),
            pltpu.VMEM((2, 16, 128), BF16),
            pltpu.VMEM((2, 2, 16, 16, 128), BF16),
            pltpu.VMEM((2, 4, 32, 512), BF16),
            pltpu.VMEM((2, 3, 32, 512), BF16),
            pltpu.VMEM((32, 512), F32),
            pltpu.VMEM((128, 256), BF16),
            pltpu.VMEM((256, 256), BF16),
            pltpu.VMEM((1, 128), F32),
            pltpu.VMEM((3, 1, 128), F32),
            pltpu.VMEM((1, 128), F32),
            pltpu.VMEM((31, 1, 128), F32),
            pltpu.VMEM((8, 128), F32),
            pltpu.SemaphoreType.DMA((TILES // LOAD,)),
            pltpu.SemaphoreType.DMA((STAGES,)),
            pltpu.SemaphoreType.DMA((STAGES,)),
        ],
        compiler_params=pltpu.CompilerParams(collective_id=0, has_side_effects=True),
    )(
        tile_rows,
        tile_cols,
        primal_step.reshape(1),
        dual_step.reshape(1),
        tile_values,
        objective,
        demand,
    )
    return pl.pallas_call(
        hand_over, out_shape=shapes, in_specs=[vmem, vmem], out_specs=(vmem, vmem)
    )(*results)


def solution(mesh):
    devices = mesh.devices.reshape(mesh.shape["grp"], 2, 4, 4, 2)
    return jax.shard_map(
        on_device,
        mesh=Mesh(devices, AXES),
        in_specs=(P(WIDE, None, "grp"), P(WIDE), P(WIDE), P(WIDE, "grp"), P(WIDE, "grp"), P(), P()),
        out_specs=(P(WIDE, "grp"), P(WIDE, "grp")),
        check_vma=False,
    )
```

```python
import functools

import jax
import jax.numpy as jnp
from jax import lax
from jax.experimental import pallas as pl
from jax.experimental.pallas import tpu as pltpu
from jax.sharding import Mesh
from jax.sharding import PartitionSpec as P

AXES = ("grp", "zh", "y", "x", "core")
WIDE = AXES[1:]
EPSILON = 1e-06
MESH = pl.DeviceIdType.MESH
F32 = jnp.float32
BF16 = jnp.bfloat16
TILES = 16
CHUNK = 4
LOAD = 2

NAMES, SCAL_X, SCAL_PLANE = range(3)
UP_X, UP_PLANE = 3, 6
UP_CORE, UP_ALL, DOWN_ALL, DOWN_CORE = 9, 11, 13, 15
STAGES = 17


def offsets():
    found = []
    for og in range(2):
        for oz in range(2):
            for oy in range(4):
                for ox in range(4):
                    hops = (1 if og else 2 * oz) + min(oy, 4 - oy) + min(ox, 4 - ox)
                    found.append((hops, og, oz, oy, ox))
    return [entry[1:] for entry in sorted(found, reverse=True) if entry[0]]


CHIPS = offsets()
PLANE = [(og, oz, oy, oc) for og, oz, oy, ox in CHIPS if ox == 0 for oc in range(2)]
PLANE.append((0, 0, 0, 1))


def iota(shape, dim):
    return lax.broadcasted_iota(jnp.int32, shape, dim)


def one_hot(condition):
    return jnp.where(condition, 1.0, 0.0).astype(BF16)


def split(value):
    high = value.astype(BF16)
    return high, (value - high.astype(F32)).astype(BF16)


def wait_bytes(ref, sem):
    pltpu.make_async_copy(ref, ref, sem).wait()


def dot(left, right):
    return lax.dot_general(left, right, (((1,), (0,)), ((), ())), preferred_element_type=F32)


def dot_nt(left, right):
    return lax.dot_general(left, right, (((1,), (1,)), ((), ())), preferred_element_type=F32)


def kernel(
    rows_hbm,
    cols_hbm,
    primal_step,
    dual_step,
    tiles_hbm,
    objective_hbm,
    demand_hbm,
    primal_out,
    dual_out,
    tile_rows,
    tile_cols,
    objective,
    demand,
    tiles,
    flipped,
    names,
    names_in,
    row_parts,
    col_parts,
    buf_a,
    send_b,
    recv_b,
    buf_c,
    send_c,
    recv_c,
    pay,
    rows,
    sel,
    recv_a,
    picked,
    hot_up,
    hot_core,
    hot_down,
    scal,
    scal_x,
    scal_out,
    scal_in,
    demand8,
    tile_sem,
    small_sem,
    send_sem,
    recv_sem,
):
    g, zh, y, x, c = (lax.axis_index(axis) for axis in AXES)
    slot_me = (zh * 4 + y) * 2 + c
    first_col = ((slot_me >> 1) * 4 + x) * 2 + c
    first_col = first_col * objective.shape[0]

    def x_device(step):
        return (g, zh, y, lax.rem(x + step, 4), c)

    def plane(entry):
        og, oz, oy, oc = entry
        return (
            lax.rem(g + og, 2),
            lax.rem(zh + oz, 2),
            lax.rem(y + oy, 4),
            lax.rem(c + oc, 2),
        )

    def chip(entry):
        og, oz, oy, ox = entry
        return (
            lax.rem(g + og, 2),
            lax.rem(zh + oz, 2),
            lax.rem(y + oy, 4),
            lax.rem(x + ox, 4),
        )

    other_core = (g, zh, y, x, 1 - c)
    chip_me = (zh * 4 + y) * 4 + x

    def send(src, dst, stage, device):
        pltpu.make_async_remote_copy(
            src_ref=src,
            dst_ref=dst,
            send_sem=send_sem.at[stage],
            recv_sem=recv_sem.at[stage],
            device_id=device,
            device_id_type=MESH,
        ).start()

    small = [
        pltpu.make_async_copy(src, dst, small_sem.at[i])
        for i, (src, dst) in enumerate(
            (
                (cols_hbm, tile_cols),
                (rows_hbm, tile_rows),
                (demand_hbm, demand),
                (objective_hbm, objective),
            )
        )
    ]
    for copy in small:
        copy.start()

    def load(chunk):
        part = pl.ds(chunk * LOAD, LOAD)
        return pltpu.make_async_copy(tiles_hbm.at[part], tiles.at[part], tile_sem.at[chunk])

    for chunk in range(TILES // LOAD):
        load(chunk).start()

    barrier = pltpu.get_barrier_semaphore()
    for step in range(1, 4):
        pl.semaphore_signal(barrier, inc=1, device_id=x_device(step), device_id_type=MESH)
    for entry in PLANE:
        pg, pz, py, pc = plane(entry)
        pl.semaphore_signal(barrier, inc=1, device_id=(pg, pz, py, x, pc), device_id_type=MESH)

    def column_of(k):
        return tile_cols[k] - first_col

    ones_row = jnp.ones((16, 256), BF16)
    for chunk in range(TILES // LOAD):
        load(chunk).wait()
        for k in range(chunk * LOAD, (chunk + 1) * LOAD):
            block = tiles[k]
            turned = block.T
            flipped[k] = turned
            row_parts[k : k + 1, :] = dot(ones_row, jnp.abs(turned))[0:1]
            col_parts[k : k + 1, :] = jnp.sum(
                jnp.abs(block).astype(F32), axis=0, keepdims=True
            )

    for copy in small:
        copy.wait()

    sub = iota((16, 128), 0)
    lane = iota((8, 128), 1)
    down = jnp.zeros((16, 128), jnp.int32)
    along = jnp.zeros((8, 128), jnp.int32)
    for k in range(TILES):
        down = jnp.where(sub == k, tile_rows[k], down)
        along = jnp.where((lane & 15) == k, tile_rows[k], along)
    names[0:16, :] = down
    names[16:24, :] = along
    demand8[0:4, :] = demand[:, 0:128]
    demand8[4:8, :] = demand[:, 128:256]

    eight = iota((8, 256), 0)
    col_total = jnp.zeros((8, 256), F32)
    for k in range(TILES):
        col_total += jnp.where(eight == column_of(k), col_parts[k : k + 1, :], 0.0)

    def stage_up(buf):
        high, low = split(row_parts[...])
        buf[0, 0:16, :] = high
        buf[0, 16:32, :] = low

    def send_up(q):
        for step in (2, 1, 3):
            send(buf_a.at[q, 0], buf_a.at[q, step], UP_X + q, x_device(step))

    def send_core(t):
        send(buf_c.at[t, 0], buf_c.at[t, 1], UP_CORE + t, other_core)

    row16 = iota((16, 512), 0) & 7

    def row_products(left, magnitude):
        def body(step, carry):
            for j in range(CHUNK):
                k = step * CHUNK + j
                block = flipped[k]
                if magnitude:
                    block = jnp.abs(block)
                mine = jnp.where(row16 == column_of(k), dot(left, block), 0.0)
                row_parts[pl.ds(k, 1), :] = jnp.sum(mine, axis=0, keepdims=True)
            return carry

        lax.fori_loop(0, TILES // CHUNK, body, 0)

    eight_wide = iota((8, 512), 0)

    def column_products(magnitude):
        def body(step, total):
            lefts = []
            for j in range(CHUNK):
                k = step * CHUNK + j
                mine = eight_wide == column_of(k)
                pieces = [
                    jnp.where(mine, picked[pl.ds(kind * 16 + k, 1), :], 0.0) for kind in range(2)
                ]
                lefts.append(jnp.concatenate(pieces, axis=0).astype(BF16))
            block = tiles[pl.ds(step * CHUNK, CHUNK)].reshape(CHUNK * 512, 256)
            if magnitude:
                block = jnp.abs(block)
            return total + dot(jnp.concatenate(lefts, axis=1), block)

        return lax.fori_loop(0, TILES // CHUNK, body, jnp.zeros((16, 256), F32))

    stage_up(buf_a.at[0])
    col_factor = 1.0 / jnp.sqrt(col_total + EPSILON)
    rounded = jnp.concatenate([col_factor, jnp.zeros_like(col_factor)], axis=0).astype(BF16)
    row_products(rounded, True)
    stage_up(buf_a.at[1])
    pl.semaphore_wait(barrier, 34)
    for step in (2, 1, 3):
        send(names, names_in.at[step - 1], NAMES, x_device(step))
    send(names, names_in.at[3], NAMES, other_core)
    send_up(0)
    send_up(1)

    wait_bytes(names_in, recv_sem.at[NAMES])
    lane_names = [names[16:17, :]] + [names_in[p, 16:17, :] for p in range(3)]
    quarter = iota((1, 128), 1) >> 5
    narrow = lane_names[3]
    for p in range(3):
        narrow = jnp.where(quarter == p, lane_names[p], narrow)
    narrow = jnp.concatenate([narrow, narrow], axis=1)
    m = iota((128, 256), 0)
    n = iota((128, 256), 1)

    def row_id(slot, index):
        return ((((slot >> 1) * 4 + x) * 2 + (slot & 1)) * 4) + index

    hot_up[...] = one_hot(
        jnp.logical_and(narrow == row_id(m >> 3, m & 3), (n >> 7) == ((m >> 2) & 1))
    )
    core_names = jnp.where(
        ((iota((1, 128), 1) >> 5) & 1) == 0, lane_names[0], names_in[3, 16:17, :]
    )
    m = iota((256, 128), 0)
    n = iota((256, 128), 1)

    def core_id(slot, index):
        return (slot * 2 + c) * 4 + index

    hot_core[...] = one_hot(
        jnp.logical_and(core_names == core_id(m >> 3, m & 3), (n >> 6) == ((m >> 2) & 1))
    )
    n16 = iota((16, 512), 1)
    ids16 = core_id(n16 >> 4, n16 & 3)
    group = (n16 >> 2) & 3
    for p, held in enumerate((names[0:16, :], names_in[3, 0:16, :])):
        named = jnp.concatenate([held] * 4, axis=1) == ids16
        for half in range(2):
            for kind in range(2):
                at = p * 64 + half * 32 + kind * 16
                hot_down[at : at + 16, :] = one_hot(
                    jnp.logical_and(named, group == kind * 2 + half)
                )

    def by_quarters(terms):
        return jnp.concatenate(
            [
                jnp.concatenate([terms[:, 0:128], terms[:, 256:384]], axis=1),
                jnp.concatenate([terms[:, 128:256], terms[:, 384:512]], axis=1),
            ],
            axis=0,
        )

    def to_owner(q):
        wait_bytes(buf_a.at[q, 1:4], recv_sem.at[UP_X + q])
        terms = by_quarters(buf_a[q].reshape(128, 512))
        send_b[q] = dot(hot_up[...], terms).reshape(16, 8, 256)
        for index, entry in enumerate(PLANE):
            pg, pz, py, pc = plane(entry)
            target = (pz * 4 + py) * 2 + pc
            lanes = pl.ds(pl.multiple_of(pg * 128, 128), 128)
            send(
                send_b.at[q, target, :, lanes],
                recv_b.at[q, index],
                UP_PLANE + q,
                (pg, pz, py, x, pc),
            )

    def own_total(q):
        mine = send_b[q, slot_me]
        mine = jnp.where(g == 0, mine[:, 0:128], mine[:, 128:256])
        wait_bytes(recv_b.at[q], recv_sem.at[UP_PLANE + q])
        return mine + jnp.sum(recv_b[q], axis=0)

    def to_owner_direct(t):
        wait_bytes(buf_c.at[t, 1], recv_sem.at[UP_CORE + t])
        terms = by_quarters(buf_c[t].reshape(64, 512))
        send_c[t] = dot(hot_core[...], terms).reshape(32, 8, 256)
        for index, entry in enumerate(CHIPS):
            pg, pz, py, px = chip(entry)
            target = (pz * 4 + py) * 4 + px
            lanes = pl.ds(pl.multiple_of(pg * 128, 128), 128)
            send(
                send_c.at[t, target, :, lanes],
                recv_c.at[t, index],
                UP_ALL + t,
                (pg, pz, py, px, c),
            )

    def own_total_direct(t):
        mine = send_c[t, chip_me]
        mine = jnp.where(g == 0, mine[:, 0:128], mine[:, 128:256])
        wait_bytes(recv_c.at[t], recv_sem.at[UP_ALL + t])
        return mine + jnp.sum(recv_c[t], axis=0)

    def to_holders(t, first, second):
        pay[t] = jnp.concatenate([first, second], axis=0).astype(BF16)
        for entry in CHIPS:
            pg, pz, py, px = chip(entry)
            send(pay.at[t], rows.at[t, g, chip_me], DOWN_ALL + t, (pg, pz, py, px, c))
        pltpu.make_async_copy(
            pay.at[t], rows.at[t, g, chip_me], recv_sem.at[DOWN_ALL + t]
        ).start()
        wait_bytes(rows.at[t], recv_sem.at[DOWN_ALL + t])
        for half in range(2):
            chosen = dot(hot_down[...], rows[t, half].reshape(512, 128)).astype(BF16)
            for p in range(2):
                for quarter in range(2):
                    at = (half * 2 + quarter) * 128
                    begin = p * 64 + quarter * 32
                    sel[t, p, :, at : at + 128] = chosen[begin : begin + 32]
        send(sel.at[t, 1], recv_a.at[t], DOWN_CORE + t, other_core)
        own = sel[t, 0].astype(F32)
        wait_bytes(recv_a.at[t], recv_sem.at[DOWN_CORE + t])
        picked[...] = own + recv_a[t].astype(F32)

    to_owner(0)
    to_owner(1)
    first_sum = own_total(0)
    second_sum = own_total(1)
    row_first = 1.0 / jnp.sqrt(first_sum + EPSILON)
    row_factor = row_first / jnp.sqrt(row_first * second_sum + EPSILON)
    to_holders(0, row_first, row_factor)

    sums = column_products(True)
    col_next = col_factor / jnp.sqrt(col_factor * sums[0:8] + EPSILON)
    col_abs = col_next * sums[8:16]
    primal_rate = primal_step[()] / (col_abs + EPSILON)
    cost_scaled = col_next * objective[...]
    demand_scaled = row_factor * demand8[...]

    def squares(value):
        return jnp.sum(jnp.sum(value * value, axis=0, keepdims=True), axis=1, keepdims=True)

    scal[...] = jnp.where(iota((1, 128), 1) < 64, squares(cost_scaled), squares(demand_scaled))
    for step in (2, 1, 3):
        send(scal, scal_x.at[step - 1], SCAL_X, x_device(step))

    def high_low(value):
        top = value.astype(BF16).astype(F32)
        return jnp.concatenate([top, value - top], axis=0).astype(BF16)

    row_products(high_low(col_next), True)
    stage_up(buf_a.at[2])
    send_up(2)
    unit = jnp.maximum(-primal_rate * cost_scaled, 0.0)
    row_products(high_low(col_next * (2.0 * unit)), False)
    stage_up(buf_c.at[0])
    send_core(0)

    wait_bytes(scal_x, recv_sem.at[SCAL_X])
    scal_out[...] = scal[...] + scal_x[0] + scal_x[1] + scal_x[2]
    for index, entry in enumerate(PLANE):
        pg, pz, py, pc = plane(entry)
        send(scal_out, scal_in.at[index], SCAL_PLANE, (pg, pz, py, x, pc))
    to_owner_direct(0)
    to_owner(2)
    wait_bytes(scal_in, recv_sem.at[SCAL_PLANE])
    both_squares = scal_out[...] + jnp.sum(scal_in[...], axis=0)
    wide_count = 64
    cost_gain = 1.0 / jnp.sqrt(both_squares[:, 0:1] / (8 * wide_count * 512) + EPSILON)
    demand_gain = 1.0 / jnp.sqrt(both_squares[:, 64:65] / (4 * wide_count * 512) + EPSILON)
    primal = cost_gain * unit
    cost_hat = cost_scaled * cost_gain
    demand_hat = demand_scaled * demand_gain

    dual_rate = dual_step[()] / (row_factor * own_total(2) + EPSILON)
    dual = dual_rate * (demand_hat - row_factor * (own_total_direct(0) * cost_gain))
    weighted = row_factor * dual.astype(BF16).astype(F32)
    top = weighted.astype(BF16).astype(F32)
    to_holders(1, top, weighted - top)

    sums = column_products(False)
    pulled = col_next * (sums[0:8] + sums[8:16])
    primal_next = jnp.maximum(primal - primal_rate * (cost_hat - pulled), 0.0)
    primal_out[...] = primal_next
    bar = (2.0 * primal_next - primal).astype(BF16).astype(F32)
    row_products(high_low(col_next * bar), False)
    stage_up(buf_c.at[1])
    send_core(1)
    to_owner_direct(1)
    dual_next = dual + dual_rate * (demand_hat - row_factor * own_total_direct(1))
    dual_out[:, 0:128] = dual_next[0:4]
    dual_out[:, 128:256] = dual_next[4:8]

    wait_bytes(names_in, send_sem.at[NAMES])
    wait_bytes(scal_x, send_sem.at[SCAL_X])
    wait_bytes(scal_in, send_sem.at[SCAL_PLANE])
    for q in range(3):
        wait_bytes(buf_a.at[q, 1:4], send_sem.at[UP_X + q])
        wait_bytes(recv_b.at[q], send_sem.at[UP_PLANE + q])
    for t in range(2):
        wait_bytes(buf_c.at[t, 1], send_sem.at[UP_CORE + t])
        wait_bytes(recv_c.at[t], send_sem.at[UP_ALL + t])
        wait_bytes(recv_c.at[t], send_sem.at[DOWN_ALL + t])
        wait_bytes(recv_a.at[t], send_sem.at[DOWN_CORE + t])


def hand_over(primal, dual, primal_out, dual_out):
    primal_out[...] = primal[...]
    dual_out[...] = dual[...]


def on_device(tile_values, tile_rows, tile_cols, objective, demand, primal_step, dual_step):
    vmem = pl.BlockSpec(memory_space=pltpu.VMEM)
    hbm = pl.BlockSpec(memory_space=pl.ANY)
    smem = pl.BlockSpec(memory_space=pltpu.SMEM)
    shapes = (
        jax.ShapeDtypeStruct(objective.shape, F32),
        jax.ShapeDtypeStruct(demand.shape, F32),
    )
    results = pl.pallas_call(
        kernel,
        out_shape=tuple(pltpu.VMEM(shape.shape, F32) for shape in shapes),
        in_specs=[hbm, hbm, smem, smem, hbm, hbm, hbm],
        out_specs=(vmem, vmem),
        scratch_shapes=[
            pltpu.SMEM(tile_rows.shape, jnp.int32),
            pltpu.SMEM(tile_cols.shape, jnp.int32),
            pltpu.VMEM(objective.shape, F32),
            pltpu.VMEM(demand.shape, F32),
            pltpu.VMEM((TILES, 512, 256), BF16),
            pltpu.VMEM((TILES, 256, 512), BF16),
            pltpu.VMEM((24, 128), jnp.int32),
            pltpu.VMEM((4, 24, 128), jnp.int32),
            pltpu.VMEM((16, 512), F32),
            pltpu.VMEM((16, 256), F32),
            pltpu.VMEM((3, 4, 32, 512), BF16),
            pltpu.VMEM((3, 16, 8, 256), F32),
            pltpu.VMEM((3, 31, 8, 128), F32),
            pltpu.VMEM((2, 2, 32, 512), BF16),
            pltpu.VMEM((2, 32, 8, 256), F32),
            pltpu.VMEM((2, 63, 8, 128), F32),
            pltpu.VMEM((2, 16, 128), BF16),
            pltpu.VMEM((2, 2, 32, 16, 128), BF16),
            pltpu.VMEM((2, 2, 32, 512), BF16),
            pltpu.VMEM((2, 32, 512), BF16),
            pltpu.VMEM((32, 512), F32),
            pltpu.VMEM((128, 256), BF16),
            pltpu.VMEM((256, 128), BF16),
            pltpu.VMEM((128, 512), BF16),
            pltpu.VMEM((1, 128), F32),
            pltpu.VMEM((3, 1, 128), F32),
            pltpu.VMEM((1, 128), F32),
            pltpu.VMEM((31, 1, 128), F32),
            pltpu.VMEM((8, 128), F32),
            pltpu.SemaphoreType.DMA((TILES // LOAD,)),
            pltpu.SemaphoreType.DMA((4,)),
            pltpu.SemaphoreType.DMA((STAGES,)),
            pltpu.SemaphoreType.DMA((STAGES,)),
        ],
        compiler_params=pltpu.CompilerParams(collective_id=0, has_side_effects=True),
    )(
        tile_rows,
        tile_cols,
        primal_step,
        dual_step,
        tile_values,
        objective,
        demand,
    )
    results = [pltpu.with_memory_space_constraint(r, pltpu.VMEM) for r in results]
    return pl.pallas_call(
        hand_over, out_shape=shapes, in_specs=[vmem, vmem], out_specs=(vmem, vmem)
    )(*results)


def solution(mesh):
    devices = mesh.devices.reshape(mesh.shape["grp"], 2, 4, 4, 2)
    return jax.shard_map(
        on_device,
        mesh=Mesh(devices, AXES),
        in_specs=(P(WIDE, None, "grp"), P(WIDE), P(WIDE), P(WIDE, "grp"), P(WIDE, "grp"), P(), P()),
        out_specs=(P(WIDE, "grp"), P(WIDE, "grp")),
        check_vma=False,
    )
```

```python
import functools

import jax
import jax.numpy as jnp
from jax import lax
from jax.experimental import pallas as pl
from jax.experimental.pallas import tpu as pltpu
from jax.sharding import Mesh
from jax.sharding import PartitionSpec as P

AXES = ("grp", "zh", "y", "x", "core")
WIDE = AXES[1:]
EPSILON = 1e-06
MESH = pl.DeviceIdType.MESH
F32 = jnp.float32
BF16 = jnp.bfloat16
TILES = 16
CHUNK = 4
LOAD = 2
EARLY = 8

NAMES, NAMES_CORE, SCAL_X, SCAL_PLANE = range(4)
UP_X, UP_PLANE = 4, 6
UP_CORE, UP_ALL, DOWN_ALL, DOWN_CORE = 8, 11, 14, 16
STAGES = 18


def offsets():
    found = []
    for og in range(2):
        for oz in range(2):
            for oy in range(4):
                for ox in range(4):
                    hops = (1 if og else 2 * oz) + min(oy, 4 - oy) + min(ox, 4 - ox)
                    found.append((hops, og, oz, oy, ox))
    return [entry[1:] for entry in sorted(found, reverse=True) if entry[0]]


CHIPS = offsets()
PLANE = [(og, oz, oy, oc) for og, oz, oy, ox in CHIPS if ox == 0 for oc in range(2)]
PLANE.append((0, 0, 0, 1))


def iota(shape, dim):
    return lax.broadcasted_iota(jnp.int32, shape, dim)


def one_hot(condition):
    return jnp.where(condition, 1.0, 0.0).astype(BF16)


def split(value):
    high = value.astype(BF16)
    return high, (value - high.astype(F32)).astype(BF16)


def wait_bytes(ref, sem):
    pltpu.make_async_copy(ref, ref, sem).wait()


def dot(left, right):
    return lax.dot_general(left, right, (((1,), (0,)), ((), ())), preferred_element_type=F32)


def dot_nt(left, right):
    return lax.dot_general(left, right, (((1,), (1,)), ((), ())), preferred_element_type=F32)


def kernel(
    rows_hbm,
    cols_hbm,
    primal_step,
    dual_step,
    tiles_hbm,
    objective_hbm,
    demand_hbm,
    primal_out,
    dual_out,
    tile_rows,
    tile_cols,
    objective,
    demand,
    tiles,
    flipped,
    names,
    names_in,
    along_out,
    along_in,
    row_parts,
    first_parts,
    col_parts,
    buf_a,
    send_b,
    recv_b,
    buf_c,
    send_c,
    recv_c,
    pay,
    rows,
    sel,
    recv_a,
    picked,
    hot_up,
    hot_core,
    hot_down,
    scal,
    scal_x,
    scal_out,
    scal_in,
    demand8,
    tile_sem,
    small_sem,
    entered,
    send_sem,
    recv_sem,
):
    g, zh, y, x, c = (lax.axis_index(axis) for axis in AXES)
    slot_me = (zh * 4 + y) * 2 + c
    first_col = ((slot_me >> 1) * 4 + x) * 2 + c
    first_col = first_col * objective.shape[0]

    def x_device(step):
        return (g, zh, y, lax.rem(x + step, 4), c)

    def plane(entry):
        og, oz, oy, oc = entry
        return (
            lax.rem(g + og, 2),
            lax.rem(zh + oz, 2),
            lax.rem(y + oy, 4),
            lax.rem(c + oc, 2),
        )

    def chip(entry):
        og, oz, oy, ox = entry
        return (
            lax.rem(g + og, 2),
            lax.rem(zh + oz, 2),
            lax.rem(y + oy, 4),
            lax.rem(x + ox, 4),
        )

    other_core = (g, zh, y, x, 1 - c)
    chip_me = (zh * 4 + y) * 4 + x

    def send(src, dst, stage, device):
        pltpu.make_async_remote_copy(
            src_ref=src,
            dst_ref=dst,
            send_sem=send_sem.at[stage],
            recv_sem=recv_sem.at[stage],
            device_id=device,
            device_id_type=MESH,
        ).start()

    small = [
        pltpu.make_async_copy(src, dst, small_sem.at[i])
        for i, (src, dst) in enumerate(
            (
                (cols_hbm, tile_cols),
                (rows_hbm, tile_rows),
                (demand_hbm, demand),
                (objective_hbm, objective),
            )
        )
    ]
    for copy in small:
        copy.start()

    def load(chunk):
        part = pl.ds(chunk * LOAD, LOAD)
        return pltpu.make_async_copy(tiles_hbm.at[part], tiles.at[part], tile_sem.at[chunk])

    for chunk in range(TILES // LOAD):
        load(chunk).start()

    barrier = pltpu.get_barrier_semaphore()
    for step in range(1, 4):
        pl.semaphore_signal(barrier, inc=1, device_id=x_device(step), device_id_type=MESH)
    for entry in PLANE:
        pg, pz, py, pc = plane(entry)
        pl.semaphore_signal(barrier, inc=1, device_id=(pg, pz, py, x, pc), device_id_type=MESH)

    def column_of(k):
        return tile_cols[k] - first_col

    for chunk in range(TILES // LOAD):
        load(chunk).wait()
        for k in range(chunk * LOAD, (chunk + 1) * LOAD):
            block = tiles[k]
            if k < EARLY:
                flipped[k] = block.T
            col_parts[k : k + 1, :] = jnp.sum(
                jnp.abs(block).astype(F32), axis=0, keepdims=True
            )

    for copy in small:
        copy.wait()

    sub = iota((16, 128), 0)
    lane = iota((8, 128), 1)
    down = jnp.zeros((16, 128), jnp.int32)
    along = jnp.zeros((8, 128), jnp.int32)
    for k in range(TILES):
        down = jnp.where(sub == k, tile_rows[k], down)
        along = jnp.where((lane & 15) == k, tile_rows[k], along)
    names[0:16, :] = down
    names[16:24, :] = along
    along_out[...] = along[0:1]
    demand8[0:4, :] = demand[:, 0:128]
    demand8[4:8, :] = demand[:, 128:256]

    eight = iota((8, 256), 0)
    col_total = jnp.zeros((8, 256), F32)
    for k in range(TILES):
        col_total += jnp.where(eight == column_of(k), col_parts[k : k + 1, :], 0.0)

    def stage_up(buf, parts):
        high, low = split(parts[...])
        buf[0, 0:16, :] = high
        buf[0, 16:32, :] = low

    def send_up(q):
        for step in (2, 1, 3):
            send(buf_a.at[q, 0], buf_a.at[q, step], UP_X + q, x_device(step))

    def send_core(t):
        send(buf_c.at[t, 0], buf_c.at[t, 1], UP_CORE + t, other_core)

    row16 = iota((16, 512), 0) & 7

    def row_products(left, magnitude):
        def body(step, carry):
            for j in range(CHUNK):
                k = step * CHUNK + j
                block = flipped[k]
                if magnitude:
                    block = jnp.abs(block)
                mine = jnp.where(row16 == column_of(k), dot(left, block), 0.0)
                row_parts[pl.ds(k, 1), :] = jnp.sum(mine, axis=0, keepdims=True)
            return carry

        lax.fori_loop(0, TILES // CHUNK, body, 0)

    def column_products(magnitude):
        def body(step, total):
            lefts = []
            for j in range(CHUNK):
                k = step * CHUNK + j
                mine = eight_wide == column_of(k)
                pieces = [
                    jnp.where(mine, picked[pl.ds(kind * 16 + k, 1), :], 0.0) for kind in range(2)
                ]
                lefts.append(jnp.concatenate(pieces, axis=0).astype(BF16))
            block = tiles[pl.ds(step * CHUNK, CHUNK)].reshape(CHUNK * 512, 256)
            if magnitude:
                block = jnp.abs(block)
            return total + dot(jnp.concatenate(lefts, axis=1), block)

        return lax.fori_loop(0, TILES // CHUNK, body, jnp.zeros((16, 256), F32))

    col_factor = 1.0 / jnp.sqrt(col_total + EPSILON)
    left = jnp.concatenate([col_factor, jnp.where(eight == 0, 1.0, 0.0)], axis=0).astype(BF16)
    eight_wide = iota((8, 512), 0)

    def both_sums(turned, step, carry):
        for j in range(CHUNK):
            k = step * CHUNK + j
            if turned:
                sums = dot(left, jnp.abs(flipped[k]))
            else:
                sums = dot_nt(left, jnp.abs(tiles[k]))
            mine = jnp.where(eight_wide == column_of(k), sums[0:8], 0.0)
            row_parts[pl.ds(k, 1), :] = jnp.sum(mine, axis=0, keepdims=True)
            first_parts[pl.ds(k, 1), :] = sums[8:9]
        return carry

    lax.fori_loop(0, EARLY // CHUNK, functools.partial(both_sums, True), 0)
    lax.fori_loop(EARLY // CHUNK, TILES // CHUNK, functools.partial(both_sums, False), 0)
    stage_up(buf_c.at[0], row_parts)
    stage_up(buf_a.at[0], first_parts)
    pl.semaphore_wait(barrier, 34)
    for step in (2, 1, 3):
        pl.semaphore_signal(entered, inc=1, device_id=x_device(step), device_id_type=MESH)
    send(names, names_in, NAMES_CORE, other_core)
    send_core(0)
    send_up(0)
    for step in (2, 1, 3):
        send(along_out, along_in.at[step - 1], NAMES, x_device(step))

    def core_tables():
        core_names = jnp.where(
            ((iota((1, 128), 1) >> 5) & 1) == 0, names[16:17, :], names_in[16:17, :]
        )
        m = iota((256, 128), 0)
        n = iota((256, 128), 1)
        hot_core[...] = one_hot(
            jnp.logical_and(core_names == core_id(m >> 3, m & 3), (n >> 6) == ((m >> 2) & 1))
        )

    def core_id(slot, index):
        return (slot * 2 + c) * 4 + index

    def x_tables():
        quarter = iota((1, 128), 1) >> 5
        narrow = names[16:17, :]
        for p in range(3):
            narrow = jnp.where(quarter == p + 1, along_in[p], narrow)
        narrow = jnp.concatenate([narrow, narrow], axis=1)
        m = iota((128, 256), 0)
        n = iota((128, 256), 1)
        slot = m >> 3
        ids = ((((slot >> 1) * 4 + x) * 2 + (slot & 1)) * 4) + (m & 3)
        hot_up[...] = one_hot(jnp.logical_and(narrow == ids, (n >> 7) == ((m >> 2) & 1)))

    def down_tables():
        n16 = iota((16, 512), 1)
        ids16 = core_id(n16 >> 4, n16 & 3)
        group = (n16 >> 2) & 3
        for p, held in enumerate((names[0:16, :], names_in[0:16, :])):
            named = jnp.concatenate([held] * 4, axis=1) == ids16
            for half in range(2):
                for kind in range(2):
                    at = p * 64 + half * 32 + kind * 16
                    hot_down[at : at + 16, :] = one_hot(
                        jnp.logical_and(named, group == kind * 2 + half)
                    )

    def by_quarters(terms):
        return jnp.concatenate(
            [
                jnp.concatenate([terms[:, 0:128], terms[:, 256:384]], axis=1),
                jnp.concatenate([terms[:, 128:256], terms[:, 384:512]], axis=1),
            ],
            axis=0,
        )

    def to_owner(q):
        wait_bytes(buf_a.at[q, 1:4], recv_sem.at[UP_X + q])
        terms = by_quarters(buf_a[q].reshape(128, 512))
        send_b[q] = dot(hot_up[...], terms).reshape(16, 8, 256)
        for index, entry in enumerate(PLANE):
            pg, pz, py, pc = plane(entry)
            target = (pz * 4 + py) * 2 + pc
            lanes = pl.ds(pl.multiple_of(pg * 128, 128), 128)
            send(
                send_b.at[q, target, :, lanes],
                recv_b.at[q, index],
                UP_PLANE + q,
                (pg, pz, py, x, pc),
            )

    def own_total(q):
        mine = send_b[q, slot_me]
        mine = jnp.where(g == 0, mine[:, 0:128], mine[:, 128:256])
        wait_bytes(recv_b.at[q], recv_sem.at[UP_PLANE + q])
        return mine + jnp.sum(recv_b[q], axis=0)

    def to_owner_direct(t):
        wait_bytes(buf_c.at[t, 1], recv_sem.at[UP_CORE + t])
        terms = by_quarters(buf_c[t].reshape(64, 512))
        send_c[t] = dot(hot_core[...], terms).reshape(32, 8, 256)
        for index, entry in enumerate(CHIPS):
            pg, pz, py, px = chip(entry)
            target = (pz * 4 + py) * 4 + px
            lanes = pl.ds(pl.multiple_of(pg * 128, 128), 128)
            send(
                send_c.at[t, target, :, lanes],
                recv_c.at[t, index],
                UP_ALL + t,
                (pg, pz, py, px, c),
            )

    def own_total_direct(t):
        mine = send_c[t, chip_me]
        mine = jnp.where(g == 0, mine[:, 0:128], mine[:, 128:256])
        wait_bytes(recv_c.at[t], recv_sem.at[UP_ALL + t])
        return mine + jnp.sum(recv_c[t], axis=0)

    def to_holders(t, first, second):
        pay[t] = jnp.concatenate([first, second], axis=0).astype(BF16)
        for entry in CHIPS:
            pg, pz, py, px = chip(entry)
            send(pay.at[t], rows.at[t, g, chip_me], DOWN_ALL + t, (pg, pz, py, px, c))
        pltpu.make_async_copy(
            pay.at[t], rows.at[t, g, chip_me], recv_sem.at[DOWN_ALL + t]
        ).start()
        wait_bytes(rows.at[t], recv_sem.at[DOWN_ALL + t])
        for half in range(2):
            chosen = dot(hot_down[...], rows[t, half].reshape(512, 128)).astype(BF16)
            for p in range(2):
                for quarter in range(2):
                    at = (half * 2 + quarter) * 128
                    begin = p * 64 + quarter * 32
                    sel[t, p, :, at : at + 128] = chosen[begin : begin + 32]
        send(sel.at[t, 1], recv_a.at[t], DOWN_CORE + t, other_core)
        own = sel[t, 0].astype(F32)
        wait_bytes(recv_a.at[t], recv_sem.at[DOWN_CORE + t])
        picked[...] = own + recv_a[t].astype(F32)

    wait_bytes(names_in, recv_sem.at[NAMES_CORE])
    core_tables()
    pl.semaphore_wait(entered, 3)
    to_owner_direct(0)
    wait_bytes(along_in, recv_sem.at[NAMES])
    x_tables()
    to_owner(0)
    down_tables()

    def turn(k, carry):
        flipped[k] = tiles[k].T
        return carry

    lax.fori_loop(EARLY, TILES, turn, 0)
    second_sum = own_total_direct(0)
    first_sum = own_total(0)
    row_first = 1.0 / jnp.sqrt(first_sum + EPSILON)
    row_factor = row_first / jnp.sqrt(row_first * second_sum + EPSILON)
    to_holders(0, row_first, row_factor)

    sums = column_products(True)
    col_next = col_factor / jnp.sqrt(col_factor * sums[0:8] + EPSILON)
    col_abs = col_next * sums[8:16]
    primal_rate = primal_step[()] / (col_abs + EPSILON)
    cost_scaled = col_next * objective[...]
    demand_scaled = row_factor * demand8[...]

    def squares(value):
        return jnp.sum(jnp.sum(value * value, axis=0, keepdims=True), axis=1, keepdims=True)

    scal[...] = jnp.where(iota((1, 128), 1) < 64, squares(cost_scaled), squares(demand_scaled))
    for step in (2, 1, 3):
        send(scal, scal_x.at[step - 1], SCAL_X, x_device(step))

    def high_low(value):
        top = value.astype(BF16).astype(F32)
        return jnp.concatenate([top, value - top], axis=0).astype(BF16)

    row_products(high_low(col_next), True)
    stage_up(buf_a.at[1], row_parts)
    send_up(1)
    unit = jnp.maximum(-primal_rate * cost_scaled, 0.0)
    row_products(high_low(col_next * (2.0 * unit)), False)
    stage_up(buf_c.at[1], row_parts)
    send_core(1)

    to_owner_direct(1)
    wait_bytes(scal_x, recv_sem.at[SCAL_X])
    scal_out[...] = scal[...] + scal_x[0] + scal_x[1] + scal_x[2]
    for index, entry in enumerate(PLANE):
        pg, pz, py, pc = plane(entry)
        send(scal_out, scal_in.at[index], SCAL_PLANE, (pg, pz, py, x, pc))
    to_owner(1)
    wait_bytes(scal_in, recv_sem.at[SCAL_PLANE])
    both_squares = scal_out[...] + jnp.sum(scal_in[...], axis=0)
    wide_count = 64
    cost_gain = 1.0 / jnp.sqrt(both_squares[:, 0:1] / (8 * wide_count * 512) + EPSILON)
    demand_gain = 1.0 / jnp.sqrt(both_squares[:, 64:65] / (4 * wide_count * 512) + EPSILON)
    primal = cost_gain * unit
    cost_hat = cost_scaled * cost_gain
    demand_hat = demand_scaled * demand_gain

    dual_rate = dual_step[()] / (row_factor * own_total(1) + EPSILON)
    dual = dual_rate * (demand_hat - row_factor * (own_total_direct(1) * cost_gain))
    weighted = row_factor * dual.astype(BF16).astype(F32)
    top = weighted.astype(BF16).astype(F32)
    to_holders(1, top, weighted - top)

    sums = column_products(False)
    pulled = col_next * (sums[0:8] + sums[8:16])
    primal_next = jnp.maximum(primal - primal_rate * (cost_hat - pulled), 0.0)
    primal_out[...] = primal_next
    bar = (2.0 * primal_next - primal).astype(BF16).astype(F32)
    row_products(high_low(col_next * bar), False)
    stage_up(buf_c.at[2], row_parts)
    send_core(2)
    to_owner_direct(2)
    dual_next = dual + dual_rate * (demand_hat - row_factor * own_total_direct(2))
    dual_out[:, 0:128] = dual_next[0:4]
    dual_out[:, 128:256] = dual_next[4:8]

    wait_bytes(along_in, send_sem.at[NAMES])
    wait_bytes(names_in, send_sem.at[NAMES_CORE])
    wait_bytes(scal_x, send_sem.at[SCAL_X])
    wait_bytes(scal_in, send_sem.at[SCAL_PLANE])
    for q in range(2):
        wait_bytes(buf_a.at[q, 1:4], send_sem.at[UP_X + q])
        wait_bytes(recv_b.at[q], send_sem.at[UP_PLANE + q])
    for t in range(3):
        wait_bytes(buf_c.at[t, 1], send_sem.at[UP_CORE + t])
        wait_bytes(recv_c.at[t], send_sem.at[UP_ALL + t])
    for t in range(2):
        wait_bytes(recv_c.at[t], send_sem.at[DOWN_ALL + t])
        wait_bytes(recv_a.at[t], send_sem.at[DOWN_CORE + t])


def hand_over(primal, dual, primal_out, dual_out):
    primal_out[...] = primal[...]
    dual_out[...] = dual[...]


def on_device(tile_values, tile_rows, tile_cols, objective, demand, primal_step, dual_step):
    vmem = pl.BlockSpec(memory_space=pltpu.VMEM)
    hbm = pl.BlockSpec(memory_space=pl.ANY)
    smem = pl.BlockSpec(memory_space=pltpu.SMEM)
    shapes = (
        jax.ShapeDtypeStruct(objective.shape, F32),
        jax.ShapeDtypeStruct(demand.shape, F32),
    )
    results = pl.pallas_call(
        kernel,
        out_shape=tuple(pltpu.VMEM(shape.shape, F32) for shape in shapes),
        in_specs=[hbm, hbm, smem, smem, hbm, hbm, hbm],
        out_specs=(vmem, vmem),
        scratch_shapes=[
            pltpu.SMEM(tile_rows.shape, jnp.int32),
            pltpu.SMEM(tile_cols.shape, jnp.int32),
            pltpu.VMEM(objective.shape, F32),
            pltpu.VMEM(demand.shape, F32),
            pltpu.VMEM((TILES, 512, 256), BF16),
            pltpu.VMEM((TILES, 256, 512), BF16),
            pltpu.VMEM((24, 128), jnp.int32),
            pltpu.VMEM((24, 128), jnp.int32),
            pltpu.VMEM((1, 128), jnp.int32),
            pltpu.VMEM((3, 1, 128), jnp.int32),
            pltpu.VMEM((16, 512), F32),
            pltpu.VMEM((16, 512), F32),
            pltpu.VMEM((16, 256), F32),
            pltpu.VMEM((2, 4, 32, 512), BF16),
            pltpu.VMEM((2, 16, 8, 256), F32),
            pltpu.VMEM((2, 31, 8, 128), F32),
            pltpu.VMEM((3, 2, 32, 512), BF16),
            pltpu.VMEM((3, 32, 8, 256), F32),
            pltpu.VMEM((3, 63, 8, 128), F32),
            pltpu.VMEM((2, 16, 128), BF16),
            pltpu.VMEM((2, 2, 32, 16, 128), BF16),
            pltpu.VMEM((2, 2, 32, 512), BF16),
            pltpu.VMEM((2, 32, 512), BF16),
            pltpu.VMEM((32, 512), F32),
            pltpu.VMEM((128, 256), BF16),
            pltpu.VMEM((256, 128), BF16),
            pltpu.VMEM((128, 512), BF16),
            pltpu.VMEM((1, 128), F32),
            pltpu.VMEM((3, 1, 128), F32),
            pltpu.VMEM((1, 128), F32),
            pltpu.VMEM((31, 1, 128), F32),
            pltpu.VMEM((8, 128), F32),
            pltpu.SemaphoreType.DMA((TILES // LOAD,)),
            pltpu.SemaphoreType.DMA((4,)),
            pltpu.SemaphoreType.REGULAR,
            pltpu.SemaphoreType.DMA((STAGES,)),
            pltpu.SemaphoreType.DMA((STAGES,)),
        ],
        compiler_params=pltpu.CompilerParams(collective_id=0, has_side_effects=True),
    )(
        tile_rows,
        tile_cols,
        primal_step,
        dual_step,
        tile_values,
        objective,
        demand,
    )
    results = [pltpu.with_memory_space_constraint(r, pltpu.VMEM) for r in results]
    return pl.pallas_call(
        hand_over, out_shape=shapes, in_specs=[vmem, vmem], out_specs=(vmem, vmem)
    )(*results)


def solution(mesh):
    devices = mesh.devices.reshape(mesh.shape["grp"], 2, 4, 4, 2)
    return jax.shard_map(
        on_device,
        mesh=Mesh(devices, AXES),
        in_specs=(P(WIDE, None, "grp"), P(WIDE), P(WIDE), P(WIDE, "grp"), P(WIDE, "grp"), P(), P()),
        out_specs=(P(WIDE, "grp"), P(WIDE, "grp")),
        check_vma=False,
    )
```

```python
import functools

import jax
import jax.numpy as jnp
from jax import lax
from jax.experimental import pallas as pl
from jax.experimental.pallas import tpu as pltpu
from jax.sharding import Mesh
from jax.sharding import PartitionSpec as P

AXES = ("grp", "zh", "y", "x", "core")
WIDE = AXES[1:]
EPSILON = 1e-06
MESH = pl.DeviceIdType.MESH
F32 = jnp.float32
BF16 = jnp.bfloat16
TILES = 16
CHUNK = 4
LOAD = 2
EARLY = 8

NAMES, NAMES_CORE, SCAL_X, SCAL_PLANE = range(4)
UP_X, UP_PLANE = 4, 6
UP_CORE, UP_ALL, DOWN_ALL, DOWN_CORE = 8, 11, 14, 16
STAGES = 18


def offsets():
    found = []
    for og in range(2):
        for oz in range(2):
            for oy in range(4):
                for ox in range(4):
                    hops = (1 if og else 2 * oz) + min(oy, 4 - oy) + min(ox, 4 - ox)
                    found.append((hops, og, oz, oy, ox))
    return [entry[1:] for entry in sorted(found, reverse=True) if entry[0]]


CHIPS = offsets()
PLANE = [(og, oz, oy, oc) for og, oz, oy, ox in CHIPS if ox == 0 for oc in range(2)]
PLANE.append((0, 0, 0, 1))


def iota(shape, dim):
    return lax.broadcasted_iota(jnp.int32, shape, dim)


def one_hot(condition):
    return jnp.where(condition, 1.0, 0.0).astype(BF16)


def split(value):
    high = value.astype(BF16)
    return high, (value - high.astype(F32)).astype(BF16)


def wait_bytes(ref, sem):
    pltpu.make_async_copy(ref, ref, sem).wait()


def dot(left, right):
    return lax.dot_general(left, right, (((1,), (0,)), ((), ())), preferred_element_type=F32)


def dot_nt(left, right):
    return lax.dot_general(left, right, (((1,), (1,)), ((), ())), preferred_element_type=F32)


def kernel(
    rows_hbm,
    cols_hbm,
    primal_step,
    dual_step,
    tiles_hbm,
    objective_hbm,
    demand_hbm,
    primal_out,
    dual_out,
    tile_rows,
    tile_cols,
    objective,
    demand,
    tiles,
    flipped,
    names,
    names_in,
    along_out,
    along_in,
    row_parts,
    first_parts,
    col_parts,
    buf_a,
    send_b,
    recv_b,
    buf_c,
    send_c,
    recv_c,
    send_one,
    recv_last,
    pay,
    rows,
    sel,
    recv_a,
    pay_one,
    rows_one,
    sel_one,
    recv_one,
    picked,
    hot_up,
    hot_core,
    hot_down,
    hot_one,
    scal,
    scal_x,
    scal_out,
    scal_in,
    demand8,
    tile_sem,
    small_sem,
    entered,
    send_sem,
    recv_sem,
):
    g, zh, y, x, c = (lax.axis_index(axis) for axis in AXES)
    slot_me = (zh * 4 + y) * 2 + c
    first_col = ((slot_me >> 1) * 4 + x) * 2 + c
    first_col = first_col * objective.shape[0]

    def x_device(step):
        return (g, zh, y, lax.rem(x + step, 4), c)

    def plane(entry):
        og, oz, oy, oc = entry
        return (
            lax.rem(g + og, 2),
            lax.rem(zh + oz, 2),
            lax.rem(y + oy, 4),
            lax.rem(c + oc, 2),
        )

    def chip(entry):
        og, oz, oy, ox = entry
        return (
            lax.rem(g + og, 2),
            lax.rem(zh + oz, 2),
            lax.rem(y + oy, 4),
            lax.rem(x + ox, 4),
        )

    other_core = (g, zh, y, x, 1 - c)
    chip_me = (zh * 4 + y) * 4 + x

    def send(src, dst, stage, device):
        pltpu.make_async_remote_copy(
            src_ref=src,
            dst_ref=dst,
            send_sem=send_sem.at[stage],
            recv_sem=recv_sem.at[stage],
            device_id=device,
            device_id_type=MESH,
        ).start()

    small = [
        pltpu.make_async_copy(src, dst, small_sem.at[i])
        for i, (src, dst) in enumerate(
            (
                (cols_hbm, tile_cols),
                (rows_hbm, tile_rows),
                (demand_hbm, demand),
                (objective_hbm, objective),
            )
        )
    ]
    for copy in small:
        copy.start()

    def load(chunk):
        part = pl.ds(chunk * LOAD, LOAD)
        return pltpu.make_async_copy(tiles_hbm.at[part], tiles.at[part], tile_sem.at[chunk])

    for chunk in range(TILES // LOAD):
        load(chunk).start()

    barrier = pltpu.get_barrier_semaphore()
    for step in range(1, 4):
        pl.semaphore_signal(barrier, inc=1, device_id=x_device(step), device_id_type=MESH)
    for entry in PLANE:
        pg, pz, py, pc = plane(entry)
        pl.semaphore_signal(barrier, inc=1, device_id=(pg, pz, py, x, pc), device_id_type=MESH)

    def column_of(k):
        return tile_cols[k] - first_col

    for chunk in range(TILES // LOAD):
        load(chunk).wait()
        for k in range(chunk * LOAD, (chunk + 1) * LOAD):
            block = tiles[k]
            if k < EARLY:
                flipped[k] = block.T
            col_parts[k : k + 1, :] = jnp.sum(
                jnp.abs(block).astype(F32), axis=0, keepdims=True
            )

    for copy in small:
        copy.wait()

    sub = iota((16, 128), 0)
    lane = iota((8, 128), 1)
    down = jnp.zeros((16, 128), jnp.int32)
    along = jnp.zeros((8, 128), jnp.int32)
    for k in range(TILES):
        down = jnp.where(sub == k, tile_rows[k], down)
        along = jnp.where((lane & 15) == k, tile_rows[k], along)
    names[0:16, :] = down
    names[16:24, :] = along
    along_out[...] = along[0:1]
    demand8[0:4, :] = demand[:, 0:128]
    demand8[4:8, :] = demand[:, 128:256]

    eight = iota((8, 256), 0)
    col_total = jnp.zeros((8, 256), F32)
    for k in range(TILES):
        col_total += jnp.where(eight == column_of(k), col_parts[k : k + 1, :], 0.0)

    def stage_up(buf, parts):
        high, low = split(parts[...])
        buf[0, 0:16, :] = high
        buf[0, 16:32, :] = low

    def send_up(q):
        for step in (2, 1, 3):
            send(buf_a.at[q, 0], buf_a.at[q, step], UP_X + q, x_device(step))

    def send_core(t):
        send(buf_c.at[t, 0], buf_c.at[t, 1], UP_CORE + t, other_core)

    row16 = iota((16, 512), 0) & 7

    def row_products(left, magnitude):
        def body(step, carry):
            for j in range(CHUNK):
                k = step * CHUNK + j
                block = flipped[k]
                if magnitude:
                    block = jnp.abs(block)
                mine = jnp.where(row16 == column_of(k), dot(left, block), 0.0)
                row_parts[pl.ds(k, 1), :] = jnp.sum(mine, axis=0, keepdims=True)
            return carry

        lax.fori_loop(0, TILES // CHUNK, body, 0)

    def column_products(kinds, magnitude):
        def body(step, total):
            lefts = []
            for j in range(CHUNK):
                k = step * CHUNK + j
                mine = eight_wide == column_of(k)
                pieces = [
                    jnp.where(mine, picked[pl.ds(kind * 16 + k, 1), :], 0.0)
                    for kind in range(kinds)
                ] + [jnp.zeros((8, 512), F32)] * (2 - kinds)
                lefts.append(jnp.concatenate(pieces, axis=0).astype(BF16))
            block = tiles[pl.ds(step * CHUNK, CHUNK)].reshape(CHUNK * 512, 256)
            if magnitude:
                block = jnp.abs(block)
            return total + dot(jnp.concatenate(lefts, axis=1), block)

        return lax.fori_loop(0, TILES // CHUNK, body, jnp.zeros((16, 256), F32))

    col_factor = 1.0 / jnp.sqrt(col_total + EPSILON)
    left = jnp.concatenate([col_factor, jnp.where(eight == 0, 1.0, 0.0)], axis=0).astype(BF16)
    eight_wide = iota((8, 512), 0)

    def both_sums(turned, step, carry):
        for j in range(CHUNK):
            k = step * CHUNK + j
            if turned:
                sums = dot(left, jnp.abs(flipped[k]))
            else:
                sums = dot_nt(left, jnp.abs(tiles[k]))
            mine = jnp.where(eight_wide == column_of(k), sums[0:8], 0.0)
            row_parts[pl.ds(k, 1), :] = jnp.sum(mine, axis=0, keepdims=True)
            first_parts[pl.ds(k, 1), :] = sums[8:9]
        return carry

    lax.fori_loop(0, EARLY // CHUNK, functools.partial(both_sums, True), 0)
    lax.fori_loop(EARLY // CHUNK, TILES // CHUNK, functools.partial(both_sums, False), 0)
    stage_up(buf_c.at[0], row_parts)
    stage_up(buf_a.at[0], first_parts)
    pl.semaphore_wait(barrier, 34)
    for step in (2, 1, 3):
        pl.semaphore_signal(entered, inc=1, device_id=x_device(step), device_id_type=MESH)
    send(names, names_in, NAMES_CORE, other_core)
    send_core(0)
    send_up(0)
    for step in (2, 1, 3):
        send(along_out, along_in.at[step - 1], NAMES, x_device(step))

    def core_tables():
        core_names = jnp.where(
            ((iota((1, 128), 1) >> 5) & 1) == 0, names[16:17, :], names_in[16:17, :]
        )
        m = iota((256, 128), 0)
        n = iota((256, 128), 1)
        hot_core[...] = one_hot(
            jnp.logical_and(core_names == core_id(m >> 3, m & 3), (n >> 6) == ((m >> 2) & 1))
        )

    def core_id(slot, index):
        return (slot * 2 + c) * 4 + index

    def x_tables():
        quarter = iota((1, 128), 1) >> 5
        narrow = names[16:17, :]
        for p in range(3):
            narrow = jnp.where(quarter == p + 1, along_in[p], narrow)
        narrow = jnp.concatenate([narrow, narrow], axis=1)
        m = iota((128, 256), 0)
        n = iota((128, 256), 1)
        slot = m >> 3
        ids = ((((slot >> 1) * 4 + x) * 2 + (slot & 1)) * 4) + (m & 3)
        hot_up[...] = one_hot(jnp.logical_and(narrow == ids, (n >> 7) == ((m >> 2) & 1)))

    def down_tables():
        n8 = iota((16, 256), 1)
        ids8 = core_id(n8 >> 3, n8 & 3)
        for p, held in enumerate((names[0:16, :], names_in[0:16, :])):
            named = jnp.concatenate([held] * 2, axis=1) == ids8
            for half in range(2):
                at = p * 32 + half * 16
                hot_one[at : at + 16, :] = one_hot(
                    jnp.logical_and(named, ((n8 >> 2) & 1) == half)
                )
        n16 = iota((16, 512), 1)
        ids16 = core_id(n16 >> 4, n16 & 3)
        group = (n16 >> 2) & 3
        for p, held in enumerate((names[0:16, :], names_in[0:16, :])):
            named = jnp.concatenate([held] * 4, axis=1) == ids16
            for half in range(2):
                for kind in range(2):
                    at = p * 64 + half * 32 + kind * 16
                    hot_down[at : at + 16, :] = one_hot(
                        jnp.logical_and(named, group == kind * 2 + half)
                    )

    def by_quarters(terms):
        return jnp.concatenate(
            [
                jnp.concatenate([terms[:, 0:128], terms[:, 256:384]], axis=1),
                jnp.concatenate([terms[:, 128:256], terms[:, 384:512]], axis=1),
            ],
            axis=0,
        )

    def to_owner(q):
        wait_bytes(buf_a.at[q, 1:4], recv_sem.at[UP_X + q])
        terms = by_quarters(buf_a[q].reshape(128, 512))
        send_b[q] = dot(hot_up[...], terms).reshape(16, 8, 256)
        for index, entry in enumerate(PLANE):
            pg, pz, py, pc = plane(entry)
            target = (pz * 4 + py) * 2 + pc
            lanes = pl.ds(pl.multiple_of(pg * 128, 128), 128)
            send(
                send_b.at[q, target, :, lanes],
                recv_b.at[q, index],
                UP_PLANE + q,
                (pg, pz, py, x, pc),
            )

    def own_total(q):
        mine = send_b[q, slot_me]
        mine = jnp.where(g == 0, mine[:, 0:128], mine[:, 128:256])
        wait_bytes(recv_b.at[q], recv_sem.at[UP_PLANE + q])
        return mine + jnp.sum(recv_b[q], axis=0)

    def to_owner_direct(t, out, into):
        wait_bytes(buf_c.at[t, 1], recv_sem.at[UP_CORE + t])
        terms = by_quarters(buf_c[t].reshape(64, 512))
        dense = dot(hot_core[...], terms)
        for half in range(2):
            part = dense[:, half * 128 : (half + 1) * 128].reshape(32, 8, 128)
            out[half] = part.astype(out.dtype)
        for index, entry in enumerate(CHIPS):
            pg, pz, py, px = chip(entry)
            target = (pz * 4 + py) * 4 + px
            send(out.at[pg, target], into.at[index], UP_ALL + t, (pg, pz, py, px, c))

    def own_total_direct(t, out, into):
        mine = out[g, chip_me].astype(F32)
        wait_bytes(into, recv_sem.at[UP_ALL + t])
        return mine + jnp.sum(into[...].astype(F32), axis=0)

    def to_holders(t, values, pay, rows, hot, sel, recv):
        pay[...] = values.astype(BF16)
        for entry in CHIPS:
            pg, pz, py, px = chip(entry)
            send(pay, rows.at[g, chip_me], DOWN_ALL + t, (pg, pz, py, px, c))
        pltpu.make_async_copy(pay, rows.at[g, chip_me], recv_sem.at[DOWN_ALL + t]).start()
        wait_bytes(rows, recv_sem.at[DOWN_ALL + t])
        height = pay.shape[0] * 2
        held = [
            rows[half].astype(F32).reshape(32 * pay.shape[0], 128).astype(BF16)
            for half in range(2)
        ]

        for half in range(2):
            chosen = dot(hot[...], held[half]).astype(BF16)
            for p in range(2):
                for quarter in range(2):
                    at = (half * 2 + quarter) * 128
                    begin = (p * 2 + quarter) * height
                    sel[p, :, at : at + 128] = chosen[begin : begin + height]
        send(sel.at[1], recv, DOWN_CORE + t, other_core)
        own = sel[0].astype(F32)
        wait_bytes(recv, recv_sem.at[DOWN_CORE + t])
        picked[0:height, :] = own + recv[...].astype(F32)

    wait_bytes(names_in, recv_sem.at[NAMES_CORE])
    core_tables()
    pl.semaphore_wait(entered, 3)
    to_owner_direct(0, send_c.at[0], recv_c.at[0])
    wait_bytes(along_in, recv_sem.at[NAMES])
    x_tables()
    to_owner(0)
    down_tables()

    def turn(k, carry):
        flipped[k] = tiles[k].T
        return carry

    lax.fori_loop(EARLY, TILES, turn, 0)
    second_sum = own_total_direct(0, send_c.at[0], recv_c.at[0])
    first_sum = own_total(0)
    row_first = 1.0 / jnp.sqrt(first_sum + EPSILON)
    row_factor = row_first / jnp.sqrt(row_first * second_sum + EPSILON)
    values = jnp.concatenate([row_first, row_factor], axis=0)
    to_holders(0, values, pay, rows, hot_down, sel, recv_a)

    sums = column_products(2, True)
    col_next = col_factor / jnp.sqrt(col_factor * sums[0:8] + EPSILON)
    col_abs = col_next * sums[8:16]
    primal_rate = primal_step[()] / (col_abs + EPSILON)
    cost_scaled = col_next * objective[...]
    demand_scaled = row_factor * demand8[...]

    def squares(value):
        return jnp.sum(jnp.sum(value * value, axis=0, keepdims=True), axis=1, keepdims=True)

    scal[...] = jnp.where(iota((1, 128), 1) < 64, squares(cost_scaled), squares(demand_scaled))
    for step in (2, 1, 3):
        send(scal, scal_x.at[step - 1], SCAL_X, x_device(step))

    def high_low(value):
        top = value.astype(BF16).astype(F32)
        return jnp.concatenate([top, value - top], axis=0).astype(BF16)

    row_products(high_low(col_next), True)
    stage_up(buf_a.at[1], row_parts)
    send_up(1)
    unit = jnp.maximum(-primal_rate * cost_scaled, 0.0)
    row_products(high_low(col_next * (2.0 * unit)), False)
    stage_up(buf_c.at[1], row_parts)
    send_core(1)

    to_owner_direct(1, send_c.at[1], recv_c.at[1])
    wait_bytes(scal_x, recv_sem.at[SCAL_X])
    scal_out[...] = scal[...] + scal_x[0] + scal_x[1] + scal_x[2]
    for index, entry in enumerate(PLANE):
        pg, pz, py, pc = plane(entry)
        send(scal_out, scal_in.at[index], SCAL_PLANE, (pg, pz, py, x, pc))
    to_owner(1)
    wait_bytes(scal_in, recv_sem.at[SCAL_PLANE])
    both_squares = scal_out[...] + jnp.sum(scal_in[...], axis=0)
    wide_count = 64
    cost_gain = 1.0 / jnp.sqrt(both_squares[:, 0:1] / (8 * wide_count * 512) + EPSILON)
    demand_gain = 1.0 / jnp.sqrt(both_squares[:, 64:65] / (4 * wide_count * 512) + EPSILON)
    primal = cost_gain * unit
    cost_hat = cost_scaled * cost_gain
    demand_hat = demand_scaled * demand_gain

    dual_rate = dual_step[()] / (row_factor * own_total(1) + EPSILON)
    pushed = row_factor * (own_total_direct(1, send_c.at[1], recv_c.at[1]) * cost_gain)
    dual = dual_rate * (demand_hat - pushed)
    weighted = row_factor * dual.astype(BF16).astype(F32)
    to_holders(1, weighted, pay_one, rows_one, hot_one, sel_one, recv_one)

    sums = column_products(1, False)
    pulled = col_next * sums[0:8]
    primal_next = jnp.maximum(primal - primal_rate * (cost_hat - pulled), 0.0)
    primal_out[...] = primal_next
    bar = (2.0 * primal_next - primal).astype(BF16).astype(F32)
    row_products(high_low(col_next * (bar - 3.0 * primal)), False)
    stage_up(buf_c.at[2], row_parts)
    send_core(2)
    to_owner_direct(2, send_one, recv_last)
    rest = row_factor * own_total_direct(2, send_one, recv_last)
    dual_next = dual + dual_rate * (demand_hat - (1.5 * pushed + rest))
    dual_out[:, 0:128] = dual_next[0:4]
    dual_out[:, 128:256] = dual_next[4:8]

    wait_bytes(along_in, send_sem.at[NAMES])
    wait_bytes(names_in, send_sem.at[NAMES_CORE])
    wait_bytes(scal_x, send_sem.at[SCAL_X])
    wait_bytes(scal_in, send_sem.at[SCAL_PLANE])
    for q in range(2):
        wait_bytes(buf_a.at[q, 1:4], send_sem.at[UP_X + q])
        wait_bytes(recv_b.at[q], send_sem.at[UP_PLANE + q])
    for t, into in enumerate((recv_c.at[0], recv_c.at[1], recv_last)):
        wait_bytes(buf_c.at[t, 1], send_sem.at[UP_CORE + t])
        wait_bytes(into, send_sem.at[UP_ALL + t])
    for t, (into, recv) in enumerate(((recv_c.at[0], recv_a), (recv_last, recv_one))):
        wait_bytes(into, send_sem.at[DOWN_ALL + t])
        wait_bytes(recv, send_sem.at[DOWN_CORE + t])


def hand_over(primal, dual, primal_out, dual_out):
    primal_out[...] = primal[...]
    dual_out[...] = dual[...]


def on_device(tile_values, tile_rows, tile_cols, objective, demand, primal_step, dual_step):
    vmem = pl.BlockSpec(memory_space=pltpu.VMEM)
    hbm = pl.BlockSpec(memory_space=pl.ANY)
    smem = pl.BlockSpec(memory_space=pltpu.SMEM)
    shapes = (
        jax.ShapeDtypeStruct(objective.shape, F32),
        jax.ShapeDtypeStruct(demand.shape, F32),
    )
    results = pl.pallas_call(
        kernel,
        out_shape=tuple(pltpu.VMEM(shape.shape, F32) for shape in shapes),
        in_specs=[hbm, hbm, smem, smem, hbm, hbm, hbm],
        out_specs=(vmem, vmem),
        scratch_shapes=[
            pltpu.SMEM(tile_rows.shape, jnp.int32),
            pltpu.SMEM(tile_cols.shape, jnp.int32),
            pltpu.VMEM(objective.shape, F32),
            pltpu.VMEM(demand.shape, F32),
            pltpu.VMEM((TILES, 512, 256), BF16),
            pltpu.VMEM((TILES, 256, 512), BF16),
            pltpu.VMEM((24, 128), jnp.int32),
            pltpu.VMEM((24, 128), jnp.int32),
            pltpu.VMEM((1, 128), jnp.int32),
            pltpu.VMEM((3, 1, 128), jnp.int32),
            pltpu.VMEM((16, 512), F32),
            pltpu.VMEM((16, 512), F32),
            pltpu.VMEM((16, 256), F32),
            pltpu.VMEM((2, 4, 32, 512), BF16),
            pltpu.VMEM((2, 16, 8, 256), F32),
            pltpu.VMEM((2, 31, 8, 128), F32),
            pltpu.VMEM((3, 2, 32, 512), BF16),
            pltpu.VMEM((2, 2, 32, 8, 128), F32),
            pltpu.VMEM((2, 63, 8, 128), F32),
            pltpu.VMEM((2, 32, 8, 128), BF16),
            pltpu.VMEM((63, 8, 128), BF16),
            pltpu.VMEM((16, 128), BF16),
            pltpu.VMEM((2, 32, 16, 128), BF16),
            pltpu.VMEM((2, 32, 512), BF16),
            pltpu.VMEM((32, 512), BF16),
            pltpu.VMEM((8, 128), BF16),
            pltpu.VMEM((2, 32, 8, 128), BF16),
            pltpu.VMEM((2, 16, 512), BF16),
            pltpu.VMEM((16, 512), BF16),
            pltpu.VMEM((32, 512), F32),
            pltpu.VMEM((128, 256), BF16),
            pltpu.VMEM((256, 128), BF16),
            pltpu.VMEM((128, 512), BF16),
            pltpu.VMEM((64, 256), BF16),
            pltpu.VMEM((1, 128), F32),
            pltpu.VMEM((3, 1, 128), F32),
            pltpu.VMEM((1, 128), F32),
            pltpu.VMEM((31, 1, 128), F32),
            pltpu.VMEM((8, 128), F32),
            pltpu.SemaphoreType.DMA((TILES // LOAD,)),
            pltpu.SemaphoreType.DMA((4,)),
            pltpu.SemaphoreType.REGULAR,
            pltpu.SemaphoreType.DMA((STAGES,)),
            pltpu.SemaphoreType.DMA((STAGES,)),
        ],
        compiler_params=pltpu.CompilerParams(collective_id=0, has_side_effects=True),
    )(
        tile_rows,
        tile_cols,
        primal_step,
        dual_step,
        tile_values,
        objective,
        demand,
    )
    results = [pltpu.with_memory_space_constraint(r, pltpu.VMEM) for r in results]
    return pl.pallas_call(
        hand_over, out_shape=shapes, in_specs=[vmem, vmem], out_specs=(vmem, vmem)
    )(*results)


def solution(mesh):
    devices = mesh.devices.reshape(mesh.shape["grp"], 2, 4, 4, 2)
    return jax.shard_map(
        on_device,
        mesh=Mesh(devices, AXES),
        in_specs=(P(WIDE, None, "grp"), P(WIDE), P(WIDE), P(WIDE, "grp"), P(WIDE, "grp"), P(), P()),
        out_specs=(P(WIDE, "grp"), P(WIDE, "grp")),
        check_vma=False,
    )
```

```python
import functools

import jax
import jax.numpy as jnp
from jax import lax
from jax.experimental import pallas as pl
from jax.experimental.pallas import tpu as pltpu
from jax.sharding import Mesh
from jax.sharding import PartitionSpec as P

AXES = ("grp", "zh", "y", "x", "core")
WIDE = AXES[1:]
EPSILON = 1e-06
MESH = pl.DeviceIdType.MESH
F32 = jnp.float32
BF16 = jnp.bfloat16
TILES = 16
CHUNK = 8
LOAD = 2
EARLY = 8

NAMES, NAMES_CORE, SCAL_X, SCAL_PLANE = range(4)
UP_X, UP_PLANE = 4, 6
UP_CORE, UP_ALL, DOWN_ALL, DOWN_CORE = 8, 11, 14, 16
STAGES = 18


def offsets():
    found = []
    for og in range(2):
        for oz in range(2):
            for oy in range(4):
                for ox in range(4):
                    hops = (1 if og else 2 * oz) + min(oy, 4 - oy) + min(ox, 4 - ox)
                    found.append((hops, og, oz, oy, ox))
    return [entry[1:] for entry in sorted(found, reverse=True) if entry[0]]


CHIPS = offsets()
PLANE = [(og, oz, oy, oc) for og, oz, oy, ox in CHIPS if ox == 0 for oc in range(2)]
PLANE.append((0, 0, 0, 1))


def iota(shape, dim):
    return lax.broadcasted_iota(jnp.int32, shape, dim)


def one_hot(condition):
    return jnp.where(condition, 1.0, 0.0).astype(BF16)


def split(value):
    high = value.astype(BF16)
    return high, (value - high.astype(F32)).astype(BF16)


def wait_bytes(ref, sem):
    pltpu.make_async_copy(ref, ref, sem).wait()


def dot(left, right):
    return lax.dot_general(left, right, (((1,), (0,)), ((), ())), preferred_element_type=F32)


def dot_nt(left, right):
    return lax.dot_general(left, right, (((1,), (1,)), ((), ())), preferred_element_type=F32)


def kernel(
    rows_hbm,
    cols_hbm,
    primal_step,
    dual_step,
    tiles_hbm,
    objective_hbm,
    demand_hbm,
    primal_out,
    dual_out,
    tile_rows,
    tile_cols,
    objective,
    demand,
    tiles,
    flipped,
    names,
    names_in,
    along_out,
    along_in,
    row_parts,
    first_parts,
    col_parts,
    buf_a,
    send_b,
    recv_b,
    buf_c,
    send_c,
    recv_c,
    send_one,
    recv_last,
    pay,
    rows,
    sel,
    recv_a,
    pay_one,
    rows_one,
    sel_one,
    recv_one,
    picked,
    hot_up,
    hot_core,
    hot_down,
    hot_one,
    scal,
    scal_x,
    scal_out,
    scal_in,
    demand8,
    tile_sem,
    small_sem,
    entered,
    send_sem,
    recv_sem,
):
    g, zh, y, x, c = (lax.axis_index(axis) for axis in AXES)
    slot_me = (zh * 4 + y) * 2 + c
    first_col = ((slot_me >> 1) * 4 + x) * 2 + c
    first_col = first_col * objective.shape[0]

    def x_device(step):
        return (g, zh, y, lax.rem(x + step, 4), c)

    def plane(entry):
        og, oz, oy, oc = entry
        return (
            lax.rem(g + og, 2),
            lax.rem(zh + oz, 2),
            lax.rem(y + oy, 4),
            lax.rem(c + oc, 2),
        )

    def chip(entry):
        og, oz, oy, ox = entry
        return (
            lax.rem(g + og, 2),
            lax.rem(zh + oz, 2),
            lax.rem(y + oy, 4),
            lax.rem(x + ox, 4),
        )

    other_core = (g, zh, y, x, 1 - c)
    chip_me = (zh * 4 + y) * 4 + x

    def send(src, dst, stage, device):
        pltpu.make_async_remote_copy(
            src_ref=src,
            dst_ref=dst,
            send_sem=send_sem.at[stage],
            recv_sem=recv_sem.at[stage],
            device_id=device,
            device_id_type=MESH,
        ).start()

    small = [
        pltpu.make_async_copy(src, dst, small_sem.at[i])
        for i, (src, dst) in enumerate(
            (
                (cols_hbm, tile_cols),
                (rows_hbm, tile_rows),
                (demand_hbm, demand),
                (objective_hbm, objective),
            )
        )
    ]
    for copy in small:
        copy.start()

    def load(chunk):
        part = pl.ds(chunk * LOAD, LOAD)
        return pltpu.make_async_copy(tiles_hbm.at[part], tiles.at[part], tile_sem.at[chunk])

    for chunk in range(TILES // LOAD):
        load(chunk).start()

    barrier = pltpu.get_barrier_semaphore()
    for step in range(1, 4):
        pl.semaphore_signal(barrier, inc=1, device_id=x_device(step), device_id_type=MESH)
    for entry in PLANE:
        pg, pz, py, pc = plane(entry)
        pl.semaphore_signal(barrier, inc=1, device_id=(pg, pz, py, x, pc), device_id_type=MESH)

    def column_of(k):
        return tile_cols[k] - first_col

    for chunk in range(TILES // LOAD):
        load(chunk).wait()
        for k in range(chunk * LOAD, (chunk + 1) * LOAD):
            block = tiles[k]
            if k < EARLY:
                flipped[k] = block.T
            col_parts[k : k + 1, :] = jnp.sum(
                jnp.abs(block).astype(F32), axis=0, keepdims=True
            )

    for copy in small:
        copy.wait()

    sub = iota((16, 128), 0)
    lane = iota((8, 128), 1)
    down = jnp.zeros((16, 128), jnp.int32)
    along = jnp.zeros((8, 128), jnp.int32)
    for k in range(TILES):
        down = jnp.where(sub == k, tile_rows[k], down)
        along = jnp.where((lane & 15) == k, tile_rows[k], along)
    names[0:16, :] = down
    names[16:24, :] = along
    along_out[...] = along[0:1]
    demand8[0:4, :] = demand[:, 0:128]
    demand8[4:8, :] = demand[:, 128:256]

    eight = iota((8, 256), 0)
    col_total = jnp.zeros((8, 256), F32)
    for k in range(TILES):
        col_total += jnp.where(eight == column_of(k), col_parts[k : k + 1, :], 0.0)

    def stage_up(buf, parts):
        high, low = split(parts[...])
        buf[0, 0:16, :] = high
        buf[0, 16:32, :] = low

    def send_up(q):
        for step in (2, 1, 3):
            send(buf_a.at[q, 0], buf_a.at[q, step], UP_X + q, x_device(step))

    def send_core(t):
        send(buf_c.at[t, 0], buf_c.at[t, 1], UP_CORE + t, other_core)

    row16 = iota((16, 512), 0) & 7

    def row_products(left, magnitude):
        def body(step, carry):
            for j in range(CHUNK):
                k = step * CHUNK + j
                block = flipped[k]
                if magnitude:
                    block = jnp.abs(block)
                mine = jnp.where(row16 == column_of(k), dot(left, block), 0.0)
                row_parts[pl.ds(k, 1), :] = jnp.sum(mine, axis=0, keepdims=True)
            return carry

        lax.fori_loop(0, TILES // CHUNK, body, 0)

    def column_products(kinds, magnitude):
        def body(step, total):
            lefts = []
            for j in range(CHUNK):
                k = step * CHUNK + j
                mine = eight_wide == column_of(k)
                pieces = [
                    jnp.where(mine, picked[pl.ds(kind * 16 + k, 1), :], 0.0)
                    for kind in range(kinds)
                ] + [jnp.zeros((8, 512), F32)] * (2 - kinds)
                lefts.append(jnp.concatenate(pieces, axis=0).astype(BF16))
            block = tiles[pl.ds(step * CHUNK, CHUNK)].reshape(CHUNK * 512, 256)
            if magnitude:
                block = jnp.abs(block)
            return total + dot(jnp.concatenate(lefts, axis=1), block)

        return lax.fori_loop(0, TILES // CHUNK, body, jnp.zeros((16, 256), F32))

    col_factor = 1.0 / jnp.sqrt(col_total + EPSILON)
    left = jnp.concatenate([col_factor, jnp.where(eight == 0, 1.0, 0.0)], axis=0).astype(BF16)
    eight_wide = iota((8, 512), 0)

    def both_sums(turned, step, carry):
        for j in range(CHUNK):
            k = step * CHUNK + j
            if turned:
                sums = dot(left, jnp.abs(flipped[k]))
            else:
                sums = dot_nt(left, jnp.abs(tiles[k]))
            mine = jnp.where(eight_wide == column_of(k), sums[0:8], 0.0)
            row_parts[pl.ds(k, 1), :] = jnp.sum(mine, axis=0, keepdims=True)
            first_parts[pl.ds(k, 1), :] = sums[8:9]
        return carry

    lax.fori_loop(0, EARLY // CHUNK, functools.partial(both_sums, True), 0)
    pl.semaphore_wait(barrier, 34)
    for step in (2, 1, 3):
        pl.semaphore_signal(entered, inc=1, device_id=x_device(step), device_id_type=MESH)
    lax.fori_loop(EARLY // CHUNK, TILES // CHUNK, functools.partial(both_sums, False), 0)
    stage_up(buf_c.at[0], row_parts)
    stage_up(buf_a.at[0], first_parts)
    send(names, names_in, NAMES_CORE, other_core)
    send_core(0)
    send_up(0)
    for step in (2, 1, 3):
        send(along_out, along_in.at[step - 1], NAMES, x_device(step))

    def core_tables():
        core_names = jnp.where(
            ((iota((1, 128), 1) >> 5) & 1) == 0, names[16:17, :], names_in[16:17, :]
        )
        m = iota((256, 128), 0)
        n = iota((256, 128), 1)
        hot_core[...] = one_hot(
            jnp.logical_and(core_names == core_id(m >> 3, m & 3), (n >> 6) == ((m >> 2) & 1))
        )

    def core_id(slot, index):
        return (slot * 2 + c) * 4 + index

    def x_tables():
        quarter = iota((1, 128), 1) >> 5
        narrow = names[16:17, :]
        for p in range(3):
            narrow = jnp.where(quarter == p + 1, along_in[p], narrow)
        narrow = jnp.concatenate([narrow, narrow], axis=1)
        m = iota((128, 256), 0)
        n = iota((128, 256), 1)
        slot = m >> 3
        ids = ((((slot >> 1) * 4 + x) * 2 + (slot & 1)) * 4) + (m & 3)
        hot_up[...] = one_hot(jnp.logical_and(narrow == ids, (n >> 7) == ((m >> 2) & 1)))

    def down_tables():
        n8 = iota((16, 256), 1)
        ids8 = core_id(n8 >> 3, n8 & 3)
        for p, held in enumerate((names[0:16, :], names_in[0:16, :])):
            named = jnp.concatenate([held] * 2, axis=1) == ids8
            for half in range(2):
                at = p * 32 + half * 16
                hot_one[at : at + 16, :] = one_hot(
                    jnp.logical_and(named, ((n8 >> 2) & 1) == half)
                )
        n16 = iota((16, 512), 1)
        ids16 = core_id(n16 >> 4, n16 & 3)
        group = (n16 >> 2) & 3
        for p, held in enumerate((names[0:16, :], names_in[0:16, :])):
            named = jnp.concatenate([held] * 4, axis=1) == ids16
            for half in range(2):
                for kind in range(2):
                    at = p * 64 + half * 32 + kind * 16
                    hot_down[at : at + 16, :] = one_hot(
                        jnp.logical_and(named, group == kind * 2 + half)
                    )

    def by_quarters(terms):
        return jnp.concatenate(
            [
                jnp.concatenate([terms[:, 0:128], terms[:, 256:384]], axis=1),
                jnp.concatenate([terms[:, 128:256], terms[:, 384:512]], axis=1),
            ],
            axis=0,
        )

    def to_owner(q):
        wait_bytes(buf_a.at[q, 1:4], recv_sem.at[UP_X + q])
        terms = by_quarters(buf_a[q].reshape(128, 512))
        send_b[q] = dot(hot_up[...], terms).reshape(16, 8, 256)
        for index, entry in enumerate(PLANE):
            pg, pz, py, pc = plane(entry)
            target = (pz * 4 + py) * 2 + pc
            lanes = pl.ds(pl.multiple_of(pg * 128, 128), 128)
            send(
                send_b.at[q, target, :, lanes],
                recv_b.at[q, index],
                UP_PLANE + q,
                (pg, pz, py, x, pc),
            )

    def own_total(q):
        mine = send_b[q, slot_me]
        mine = jnp.where(g == 0, mine[:, 0:128], mine[:, 128:256])
        wait_bytes(recv_b.at[q], recv_sem.at[UP_PLANE + q])
        return mine + jnp.sum(recv_b[q], axis=0)

    def to_owner_direct(t, out, into):
        wait_bytes(buf_c.at[t, 1], recv_sem.at[UP_CORE + t])
        terms = by_quarters(buf_c[t].reshape(64, 512))
        dense = dot(hot_core[...], terms)
        for half in range(2):
            part = dense[:, half * 128 : (half + 1) * 128].reshape(32, 8, 128)
            out[half] = part.astype(out.dtype)
        for index, entry in enumerate(CHIPS):
            pg, pz, py, px = chip(entry)
            target = (pz * 4 + py) * 4 + px
            send(out.at[pg, target], into.at[index], UP_ALL + t, (pg, pz, py, px, c))

    def own_total_direct(t, out, into):
        mine = out[g, chip_me].astype(F32)
        wait_bytes(into, recv_sem.at[UP_ALL + t])
        return mine + jnp.sum(into[...].astype(F32), axis=0)

    def to_holders(t, values, pay, rows, hot, sel, recv):
        pay[...] = values.astype(BF16)
        for entry in CHIPS:
            pg, pz, py, px = chip(entry)
            send(pay, rows.at[g, chip_me], DOWN_ALL + t, (pg, pz, py, px, c))
        pltpu.make_async_copy(pay, rows.at[g, chip_me], recv_sem.at[DOWN_ALL + t]).start()
        wait_bytes(rows, recv_sem.at[DOWN_ALL + t])
        height = pay.shape[0] * 2
        held = [
            rows[half].astype(F32).reshape(32 * pay.shape[0], 128).astype(BF16)
            for half in range(2)
        ]

        for half in range(2):
            chosen = dot(hot[...], held[half]).astype(BF16)
            for p in range(2):
                for quarter in range(2):
                    at = (half * 2 + quarter) * 128
                    begin = (p * 2 + quarter) * height
                    sel[p, :, at : at + 128] = chosen[begin : begin + height]
        send(sel.at[1], recv, DOWN_CORE + t, other_core)
        own = sel[0].astype(F32)
        wait_bytes(recv, recv_sem.at[DOWN_CORE + t])
        picked[0:height, :] = own + recv[...].astype(F32)

    wait_bytes(names_in, recv_sem.at[NAMES_CORE])
    core_tables()
    pl.semaphore_wait(entered, 3)
    to_owner_direct(0, send_c.at[0], recv_c.at[0])
    wait_bytes(along_in, recv_sem.at[NAMES])
    x_tables()
    to_owner(0)
    down_tables()

    def turn(k, carry):
        flipped[k] = tiles[k].T
        return carry

    lax.fori_loop(EARLY, TILES, turn, 0)
    second_sum = own_total_direct(0, send_c.at[0], recv_c.at[0])
    first_sum = own_total(0)
    row_first = 1.0 / jnp.sqrt(first_sum + EPSILON)
    row_factor = row_first / jnp.sqrt(row_first * second_sum + EPSILON)
    values = jnp.concatenate([row_first, row_factor], axis=0)
    to_holders(0, values, pay, rows, hot_down, sel, recv_a)

    sums = column_products(2, True)
    col_next = col_factor / jnp.sqrt(col_factor * sums[0:8] + EPSILON)
    col_abs = col_next * sums[8:16]
    primal_rate = primal_step[()] / (col_abs + EPSILON)
    cost_scaled = col_next * objective[...]
    demand_scaled = row_factor * demand8[...]

    def squares(value):
        return jnp.sum(jnp.sum(value * value, axis=0, keepdims=True), axis=1, keepdims=True)

    scal[...] = jnp.where(iota((1, 128), 1) < 64, squares(cost_scaled), squares(demand_scaled))
    for step in (2, 1, 3):
        send(scal, scal_x.at[step - 1], SCAL_X, x_device(step))

    def high_low(value):
        top = value.astype(BF16).astype(F32)
        return jnp.concatenate([top, value - top], axis=0).astype(BF16)

    row_products(high_low(col_next), True)
    stage_up(buf_a.at[1], row_parts)
    send_up(1)
    unit = jnp.maximum(-primal_rate * cost_scaled, 0.0)
    row_products(high_low(col_next * (2.0 * unit)), False)
    stage_up(buf_c.at[1], row_parts)
    send_core(1)

    wait_bytes(scal_x, recv_sem.at[SCAL_X])
    scal_out[...] = scal[...] + scal_x[0] + scal_x[1] + scal_x[2]
    for index, entry in enumerate(PLANE):
        pg, pz, py, pc = plane(entry)
        send(scal_out, scal_in.at[index], SCAL_PLANE, (pg, pz, py, x, pc))
    to_owner_direct(1, send_c.at[1], recv_c.at[1])
    to_owner(1)
    wait_bytes(scal_in, recv_sem.at[SCAL_PLANE])
    both_squares = scal_out[...] + jnp.sum(scal_in[...], axis=0)
    wide_count = 64
    cost_gain = 1.0 / jnp.sqrt(both_squares[:, 0:1] / (8 * wide_count * 512) + EPSILON)
    demand_gain = 1.0 / jnp.sqrt(both_squares[:, 64:65] / (4 * wide_count * 512) + EPSILON)
    primal = cost_gain * unit
    cost_hat = cost_scaled * cost_gain
    demand_hat = demand_scaled * demand_gain

    dual_rate = dual_step[()] / (row_factor * own_total(1) + EPSILON)
    pushed = row_factor * (own_total_direct(1, send_c.at[1], recv_c.at[1]) * cost_gain)
    dual = dual_rate * (demand_hat - pushed)
    weighted = row_factor * dual.astype(BF16).astype(F32)
    to_holders(1, weighted, pay_one, rows_one, hot_one, sel_one, recv_one)

    sums = column_products(1, False)
    pulled = col_next * sums[0:8]
    primal_next = jnp.maximum(primal - primal_rate * (cost_hat - pulled), 0.0)
    primal_out[...] = primal_next
    bar = (2.0 * primal_next - primal).astype(BF16).astype(F32)
    row_products(high_low(col_next * (bar - 3.0 * primal)), False)
    stage_up(buf_c.at[2], row_parts)
    send_core(2)
    to_owner_direct(2, send_one, recv_last)
    rest = row_factor * own_total_direct(2, send_one, recv_last)
    dual_next = dual + dual_rate * (demand_hat - (1.5 * pushed + rest))
    dual_out[:, 0:128] = dual_next[0:4]
    dual_out[:, 128:256] = dual_next[4:8]

    wait_bytes(along_in, send_sem.at[NAMES])
    wait_bytes(names_in, send_sem.at[NAMES_CORE])
    wait_bytes(scal_x, send_sem.at[SCAL_X])
    wait_bytes(scal_in, send_sem.at[SCAL_PLANE])
    for q in range(2):
        wait_bytes(buf_a.at[q, 1:4], send_sem.at[UP_X + q])
        wait_bytes(recv_b.at[q], send_sem.at[UP_PLANE + q])
    for t, into in enumerate((recv_c.at[0], recv_c.at[1], recv_last)):
        wait_bytes(buf_c.at[t, 1], send_sem.at[UP_CORE + t])
        wait_bytes(into, send_sem.at[UP_ALL + t])
    for t, (into, recv) in enumerate(((recv_c.at[0], recv_a), (recv_last, recv_one))):
        wait_bytes(into, send_sem.at[DOWN_ALL + t])
        wait_bytes(recv, send_sem.at[DOWN_CORE + t])


def hand_over(primal, dual, primal_out, dual_out):
    primal_out[...] = primal[...]
    dual_out[...] = dual[...]


def on_device(tile_values, tile_rows, tile_cols, objective, demand, primal_step, dual_step):
    vmem = pl.BlockSpec(memory_space=pltpu.VMEM)
    hbm = pl.BlockSpec(memory_space=pl.ANY)
    smem = pl.BlockSpec(memory_space=pltpu.SMEM)
    shapes = (
        jax.ShapeDtypeStruct(objective.shape, F32),
        jax.ShapeDtypeStruct(demand.shape, F32),
    )
    results = pl.pallas_call(
        kernel,
        out_shape=tuple(pltpu.VMEM(shape.shape, F32) for shape in shapes),
        in_specs=[hbm, hbm, smem, smem, hbm, hbm, hbm],
        out_specs=(vmem, vmem),
        scratch_shapes=[
            pltpu.SMEM(tile_rows.shape, jnp.int32),
            pltpu.SMEM(tile_cols.shape, jnp.int32),
            pltpu.VMEM(objective.shape, F32),
            pltpu.VMEM(demand.shape, F32),
            pltpu.VMEM((TILES, 512, 256), BF16),
            pltpu.VMEM((TILES, 256, 512), BF16),
            pltpu.VMEM((24, 128), jnp.int32),
            pltpu.VMEM((24, 128), jnp.int32),
            pltpu.VMEM((1, 128), jnp.int32),
            pltpu.VMEM((3, 1, 128), jnp.int32),
            pltpu.VMEM((16, 512), F32),
            pltpu.VMEM((16, 512), F32),
            pltpu.VMEM((16, 256), F32),
            pltpu.VMEM((2, 4, 32, 512), BF16),
            pltpu.VMEM((2, 16, 8, 256), F32),
            pltpu.VMEM((2, 31, 8, 128), F32),
            pltpu.VMEM((3, 2, 32, 512), BF16),
            pltpu.VMEM((2, 2, 32, 8, 128), F32),
            pltpu.VMEM((2, 63, 8, 128), F32),
            pltpu.VMEM((2, 32, 8, 128), BF16),
            pltpu.VMEM((63, 8, 128), BF16),
            pltpu.VMEM((16, 128), BF16),
            pltpu.VMEM((2, 32, 16, 128), BF16),
            pltpu.VMEM((2, 32, 512), BF16),
            pltpu.VMEM((32, 512), BF16),
            pltpu.VMEM((8, 128), BF16),
            pltpu.VMEM((2, 32, 8, 128), BF16),
            pltpu.VMEM((2, 16, 512), BF16),
            pltpu.VMEM((16, 512), BF16),
            pltpu.VMEM((32, 512), F32),
            pltpu.VMEM((128, 256), BF16),
            pltpu.VMEM((256, 128), BF16),
            pltpu.VMEM((128, 512), BF16),
            pltpu.VMEM((64, 256), BF16),
            pltpu.VMEM((1, 128), F32),
            pltpu.VMEM((3, 1, 128), F32),
            pltpu.VMEM((1, 128), F32),
            pltpu.VMEM((31, 1, 128), F32),
            pltpu.VMEM((8, 128), F32),
            pltpu.SemaphoreType.DMA((TILES // LOAD,)),
            pltpu.SemaphoreType.DMA((4,)),
            pltpu.SemaphoreType.REGULAR,
            pltpu.SemaphoreType.DMA((STAGES,)),
            pltpu.SemaphoreType.DMA((STAGES,)),
        ],
        compiler_params=pltpu.CompilerParams(collective_id=0, has_side_effects=True),
    )(
        tile_rows,
        tile_cols,
        primal_step,
        dual_step,
        tile_values,
        objective,
        demand,
    )
    results = [pltpu.with_memory_space_constraint(r, pltpu.VMEM) for r in results]
    return pl.pallas_call(
        hand_over, out_shape=shapes, in_specs=[vmem, vmem], out_specs=(vmem, vmem)
    )(*results)


def solution(mesh):
    devices = mesh.devices.reshape(mesh.shape["grp"], 2, 4, 4, 2)
    return jax.shard_map(
        on_device,
        mesh=Mesh(devices, AXES),
        in_specs=(P(WIDE, None, "grp"), P(WIDE), P(WIDE), P(WIDE, "grp"), P(WIDE, "grp"), P(), P()),
        out_specs=(P(WIDE, "grp"), P(WIDE, "grp")),
        check_vma=False,
    )
```

```python
import functools

import jax
import jax.numpy as jnp
from jax import lax
from jax.experimental import pallas as pl
from jax.experimental.pallas import tpu as pltpu
from jax.sharding import Mesh
from jax.sharding import PartitionSpec as P

AXES = ("grp", "zh", "y", "x", "core")
WIDE = AXES[1:]
EPSILON = 1e-06
MESH = pl.DeviceIdType.MESH
F32 = jnp.float32
BF16 = jnp.bfloat16
TILES = 16
CHUNK = 8
LOAD = 2
EARLY = 8

NAMES, NAMES_CORE, SCAL_X, SCAL_PLANE = range(4)
UP_X, UP_PLANE = 4, 5
UP_CORE, UP_ALL, DOWN_ALL, DOWN_CORE = 6, 10, 14, 17
STAGES = 20


def offsets():
    found = []
    for og in range(2):
        for oz in range(2):
            for oy in range(4):
                for ox in range(4):
                    hops = (1 if og else 2 * oz) + min(oy, 4 - oy) + min(ox, 4 - ox)
                    found.append((hops, og, oz, oy, ox))
    return [entry[1:] for entry in sorted(found, reverse=True) if entry[0]]


CHIPS = offsets()
PLANE = [(og, oz, oy, oc) for og, oz, oy, ox in CHIPS if ox == 0 for oc in range(2)]
PLANE.append((0, 0, 0, 1))


def iota(shape, dim):
    return lax.broadcasted_iota(jnp.int32, shape, dim)


def one_hot(condition):
    return jnp.where(condition, 1.0, 0.0).astype(BF16)


def split(value):
    high = value.astype(BF16)
    return high, (value - high.astype(F32)).astype(BF16)


def wait_bytes(ref, sem):
    pltpu.make_async_copy(ref, ref, sem).wait()


def dot(left, right):
    return lax.dot_general(left, right, (((1,), (0,)), ((), ())), preferred_element_type=F32)


def dot_nt(left, right):
    return lax.dot_general(left, right, (((1,), (1,)), ((), ())), preferred_element_type=F32)


def kernel(
    rows_hbm,
    cols_hbm,
    primal_step,
    dual_step,
    tiles_hbm,
    objective_hbm,
    demand_hbm,
    primal_out,
    dual_out,
    tile_rows,
    tile_cols,
    objective,
    demand,
    tiles,
    flipped,
    names,
    names_in,
    along_out,
    along_in,
    row_parts,
    first_parts,
    col_parts,
    buf_a,
    send_b,
    recv_b,
    buf_c,
    send_c,
    recv_c,
    send_one,
    recv_last,
    pay,
    rows,
    sel,
    recv_a,
    picked,
    hot_up,
    hot_core,
    hot_down,
    scal,
    scal_x,
    scal_out,
    scal_in,
    demand8,
    tile_sem,
    small_sem,
    entered,
    send_sem,
    recv_sem,
):
    g, zh, y, x, c = (lax.axis_index(axis) for axis in AXES)
    slot_me = (zh * 4 + y) * 2 + c
    first_col = ((slot_me >> 1) * 4 + x) * 2 + c
    first_col = first_col * objective.shape[0]

    def x_device(step):
        return (g, zh, y, lax.rem(x + step, 4), c)

    def plane(entry):
        og, oz, oy, oc = entry
        return (
            lax.rem(g + og, 2),
            lax.rem(zh + oz, 2),
            lax.rem(y + oy, 4),
            lax.rem(c + oc, 2),
        )

    def chip(entry):
        og, oz, oy, ox = entry
        return (
            lax.rem(g + og, 2),
            lax.rem(zh + oz, 2),
            lax.rem(y + oy, 4),
            lax.rem(x + ox, 4),
        )

    other_core = (g, zh, y, x, 1 - c)
    chip_me = (zh * 4 + y) * 4 + x

    def send(src, dst, stage, device):
        pltpu.make_async_remote_copy(
            src_ref=src,
            dst_ref=dst,
            send_sem=send_sem.at[stage],
            recv_sem=recv_sem.at[stage],
            device_id=device,
            device_id_type=MESH,
        ).start()

    small = [
        pltpu.make_async_copy(src, dst, small_sem.at[i])
        for i, (src, dst) in enumerate(
            (
                (cols_hbm, tile_cols),
                (rows_hbm, tile_rows),
                (demand_hbm, demand),
                (objective_hbm, objective),
            )
        )
    ]
    for copy in small:
        copy.start()

    def load(chunk):
        part = pl.ds(chunk * LOAD, LOAD)
        return pltpu.make_async_copy(tiles_hbm.at[part], tiles.at[part], tile_sem.at[chunk])

    for chunk in range(TILES // LOAD):
        load(chunk).start()

    barrier = pltpu.get_barrier_semaphore()
    for step in range(1, 4):
        pl.semaphore_signal(barrier, inc=1, device_id=x_device(step), device_id_type=MESH)
    for entry in PLANE:
        pg, pz, py, pc = plane(entry)
        pl.semaphore_signal(barrier, inc=1, device_id=(pg, pz, py, x, pc), device_id_type=MESH)

    def column_of(k):
        return tile_cols[k] - first_col

    for chunk in range(TILES // LOAD):
        load(chunk).wait()
        for k in range(chunk * LOAD, (chunk + 1) * LOAD):
            block = tiles[k]
            if k < EARLY:
                flipped[k] = block.T
            col_parts[k : k + 1, :] = jnp.sum(
                jnp.abs(block).astype(F32), axis=0, keepdims=True
            )

    for copy in small:
        copy.wait()

    sub = iota((16, 128), 0)
    lane = iota((8, 128), 1)
    down = jnp.zeros((16, 128), jnp.int32)
    along = jnp.zeros((8, 128), jnp.int32)
    for k in range(TILES):
        down = jnp.where(sub == k, tile_rows[k], down)
        along = jnp.where((lane & 15) == k, tile_rows[k], along)
    names[0:16, :] = down
    names[16:24, :] = along
    along_out[...] = along[0:1]
    demand8[0:4, :] = demand[:, 0:128]
    demand8[4:8, :] = demand[:, 128:256]

    eight = iota((8, 256), 0)
    col_total = jnp.zeros((8, 256), F32)
    for k in range(TILES):
        col_total += jnp.where(eight == column_of(k), col_parts[k : k + 1, :], 0.0)

    def stage_up(buf, parts):
        high, low = split(parts[...])
        buf[0, 0:16, :] = high
        buf[0, 16:32, :] = low

    def send_up(q):
        for step in (2, 1, 3):
            send(buf_a.at[q, 0], buf_a.at[q, step], UP_X + q, x_device(step))

    def send_core(t):
        send(buf_c.at[t, 0], buf_c.at[t, 1], UP_CORE + t, other_core)

    row16 = iota((16, 512), 0) & 7

    def row_products(left, magnitude):
        def body(step, carry):
            for j in range(CHUNK):
                k = step * CHUNK + j
                block = flipped[k]
                if magnitude:
                    block = jnp.abs(block)
                mine = jnp.where(row16 == column_of(k), dot(left, block), 0.0)
                row_parts[pl.ds(k, 1), :] = jnp.sum(mine, axis=0, keepdims=True)
            return carry

        lax.fori_loop(0, TILES // CHUNK, body, 0)

    def column_products(magnitude):
        def body(step, total):
            lefts = []
            for j in range(CHUNK):
                k = step * CHUNK + j
                mine = jnp.where(eight_wide == column_of(k), picked[pl.ds(k, 1), :], 0.0)
                pieces = [mine, jnp.zeros((8, 512), F32)]
                lefts.append(jnp.concatenate(pieces, axis=0).astype(BF16))
            block = tiles[pl.ds(step * CHUNK, CHUNK)].reshape(CHUNK * 512, 256)
            if magnitude:
                block = jnp.abs(block)
            return total + dot(jnp.concatenate(lefts, axis=1), block)

        return lax.fori_loop(0, TILES // CHUNK, body, jnp.zeros((16, 256), F32))[0:8]

    col_factor = 1.0 / jnp.sqrt(col_total + EPSILON)
    left = jnp.concatenate([col_factor, jnp.where(eight == 0, 1.0, 0.0)], axis=0).astype(BF16)
    eight_wide = iota((8, 512), 0)

    def both_sums(turned, step, carry):
        for j in range(CHUNK):
            k = step * CHUNK + j
            if turned:
                sums = dot(left, jnp.abs(flipped[k]))
            else:
                sums = dot_nt(left, jnp.abs(tiles[k]))
            mine = jnp.where(eight_wide == column_of(k), sums[0:8], 0.0)
            row_parts[pl.ds(k, 1), :] = jnp.sum(mine, axis=0, keepdims=True)
            first_parts[pl.ds(k, 1), :] = sums[8:9]
        return carry

    lax.fori_loop(0, EARLY // CHUNK, functools.partial(both_sums, True), 0)
    pl.semaphore_wait(barrier, 34)
    for step in (2, 1, 3):
        pl.semaphore_signal(entered, inc=1, device_id=x_device(step), device_id_type=MESH)
    lax.fori_loop(EARLY // CHUNK, TILES // CHUNK, functools.partial(both_sums, False), 0)
    stage_up(buf_c.at[0], first_parts)
    stage_up(buf_a.at[0], row_parts)
    send(names, names_in, NAMES_CORE, other_core)
    send_core(0)
    send_up(0)
    for step in (2, 1, 3):
        send(along_out, along_in.at[step - 1], NAMES, x_device(step))

    def core_tables():
        core_names = jnp.where(
            ((iota((1, 128), 1) >> 5) & 1) == 0, names[16:17, :], names_in[16:17, :]
        )
        m = iota((256, 128), 0)
        n = iota((256, 128), 1)
        hot_core[...] = one_hot(
            jnp.logical_and(core_names == core_id(m >> 3, m & 3), (n >> 6) == ((m >> 2) & 1))
        )

    def core_id(slot, index):
        return (slot * 2 + c) * 4 + index

    def x_tables():
        quarter = iota((1, 128), 1) >> 5
        narrow = names[16:17, :]
        for p in range(3):
            narrow = jnp.where(quarter == p + 1, along_in[p], narrow)
        narrow = jnp.concatenate([narrow, narrow], axis=1)
        m = iota((128, 256), 0)
        n = iota((128, 256), 1)
        slot = m >> 3
        ids = ((((slot >> 1) * 4 + x) * 2 + (slot & 1)) * 4) + (m & 3)
        hot_up[...] = one_hot(jnp.logical_and(narrow == ids, (n >> 7) == ((m >> 2) & 1)))

    def down_tables():
        n8 = iota((16, 256), 1)
        ids8 = core_id(n8 >> 3, n8 & 3)
        for p, held in enumerate((names[0:16, :], names_in[0:16, :])):
            named = jnp.concatenate([held] * 2, axis=1) == ids8
            for half in range(2):
                at = p * 32 + half * 16
                hot_down[at : at + 16, :] = one_hot(
                    jnp.logical_and(named, ((n8 >> 2) & 1) == half)
                )

    def by_quarters(terms):
        return jnp.concatenate(
            [
                jnp.concatenate([terms[:, 0:128], terms[:, 256:384]], axis=1),
                jnp.concatenate([terms[:, 128:256], terms[:, 384:512]], axis=1),
            ],
            axis=0,
        )

    def to_owner(q):
        wait_bytes(buf_a.at[q, 1:4], recv_sem.at[UP_X + q])
        terms = by_quarters(buf_a[q].reshape(128, 512))
        send_b[q] = dot(hot_up[...], terms).reshape(16, 8, 256)
        for index, entry in enumerate(PLANE):
            pg, pz, py, pc = plane(entry)
            target = (pz * 4 + py) * 2 + pc
            lanes = pl.ds(pl.multiple_of(pg * 128, 128), 128)
            send(
                send_b.at[q, target, :, lanes],
                recv_b.at[q, index],
                UP_PLANE + q,
                (pg, pz, py, x, pc),
            )

    def own_total(q):
        mine = send_b[q, slot_me]
        mine = jnp.where(g == 0, mine[:, 0:128], mine[:, 128:256])
        wait_bytes(recv_b.at[q], recv_sem.at[UP_PLANE + q])
        return mine + jnp.sum(recv_b[q], axis=0)

    def to_owner_direct(t, out, into):
        wait_bytes(buf_c.at[t, 1], recv_sem.at[UP_CORE + t])
        terms = by_quarters(buf_c[t].reshape(64, 512))
        dense = dot(hot_core[...], terms)
        for half in range(2):
            part = dense[:, half * 128 : (half + 1) * 128].reshape(32, 8, 128)
            out[half] = part.astype(out.dtype)
        for index, entry in enumerate(CHIPS):
            pg, pz, py, px = chip(entry)
            target = (pz * 4 + py) * 4 + px
            send(out.at[pg, target], into.at[index], UP_ALL + t, (pg, pz, py, px, c))

    def own_total_direct(t, out, into):
        mine = out[g, chip_me].astype(F32)
        wait_bytes(into, recv_sem.at[UP_ALL + t])
        return mine + jnp.sum(into[...].astype(F32), axis=0)

    def gather(t, values):
        pay[t] = values.astype(BF16)
        for entry in CHIPS:
            pg, pz, py, px = chip(entry)
            send(pay.at[t], rows.at[t, g, chip_me], DOWN_ALL + t, (pg, pz, py, px, c))
        pltpu.make_async_copy(
            pay.at[t], rows.at[t, g, chip_me], recv_sem.at[DOWN_ALL + t]
        ).start()

    def pick(t):
        wait_bytes(rows.at[t], recv_sem.at[DOWN_ALL + t])
        for half in range(2):
            held = rows[t, half].astype(F32).reshape(256, 128).astype(BF16)
            chosen = dot(hot_down[...], held).astype(BF16)
            for p in range(2):
                for quarter in range(2):
                    at = (half * 2 + quarter) * 128
                    begin = (p * 2 + quarter) * 16
                    sel[t, p, :, at : at + 128] = chosen[begin : begin + 16]
        send(sel.at[t, 1], recv_a.at[t], DOWN_CORE + t, other_core)

    def picked_rows(t):
        own = sel[t, 0].astype(F32)
        wait_bytes(recv_a.at[t], recv_sem.at[DOWN_CORE + t])
        picked[...] = own + recv_a[t].astype(F32)

    wait_bytes(names_in, recv_sem.at[NAMES_CORE])
    core_tables()
    pl.semaphore_wait(entered, 3)
    to_owner_direct(0, send_c.at[0], recv_c.at[0])
    wait_bytes(along_in, recv_sem.at[NAMES])
    x_tables()
    to_owner(0)
    down_tables()

    def turn(k, carry):
        flipped[k] = tiles[k].T
        return carry

    lax.fori_loop(EARLY, TILES, turn, 0)
    row_first = 1.0 / jnp.sqrt(own_total_direct(0, send_c.at[0], recv_c.at[0]) + EPSILON)
    gather(0, row_first)
    row_factor = row_first / jnp.sqrt(row_first * own_total(0) + EPSILON)
    gather(1, row_factor)

    pick(0)
    picked_rows(0)
    sums = column_products(True)
    col_next = col_factor / jnp.sqrt(col_factor * sums + EPSILON)
    cost_scaled = col_next * objective[...]
    demand_scaled = row_factor * demand8[...]

    def squares(value):
        return jnp.sum(jnp.sum(value * value, axis=0, keepdims=True), axis=1, keepdims=True)

    scal[...] = jnp.where(iota((1, 128), 1) < 64, squares(cost_scaled), squares(demand_scaled))
    for step in (2, 1, 3):
        send(scal, scal_x.at[step - 1], SCAL_X, x_device(step))

    def high_low(value):
        top = value.astype(BF16).astype(F32)
        return jnp.concatenate([top, value - top], axis=0).astype(BF16)

    pick(1)
    row_products(high_low(col_next), True)
    stage_up(buf_c.at[1], row_parts)
    send_core(1)
    picked_rows(1)
    col_abs = col_next * column_products(True)
    primal_rate = primal_step[()] / (col_abs + EPSILON)
    to_owner_direct(1, send_c.at[1], recv_c.at[1])
    wait_bytes(scal_x, recv_sem.at[SCAL_X])
    scal_out[...] = scal[...] + scal_x[0] + scal_x[1] + scal_x[2]
    for index, entry in enumerate(PLANE):
        pg, pz, py, pc = plane(entry)
        send(scal_out, scal_in.at[index], SCAL_PLANE, (pg, pz, py, x, pc))
    unit = jnp.maximum(-primal_rate * cost_scaled, 0.0)
    row_products(high_low(col_next * (2.0 * unit)), False)
    stage_up(buf_c.at[2], row_parts)
    send_core(2)

    to_owner_direct(2, send_c.at[2], recv_c.at[2])
    wait_bytes(scal_in, recv_sem.at[SCAL_PLANE])
    both_squares = scal_out[...] + jnp.sum(scal_in[...], axis=0)
    wide_count = 64
    cost_gain = 1.0 / jnp.sqrt(both_squares[:, 0:1] / (8 * wide_count * 512) + EPSILON)
    demand_gain = 1.0 / jnp.sqrt(both_squares[:, 64:65] / (4 * wide_count * 512) + EPSILON)
    primal = cost_gain * unit
    cost_hat = cost_scaled * cost_gain
    demand_hat = demand_scaled * demand_gain

    dual_rate = dual_step[()] / (row_factor * own_total_direct(1, send_c.at[1], recv_c.at[1]) + EPSILON)
    pushed = row_factor * (own_total_direct(2, send_c.at[2], recv_c.at[2]) * cost_gain)
    dual = dual_rate * (demand_hat - pushed)
    weighted = row_factor * dual.astype(BF16).astype(F32)
    gather(2, weighted)
    pick(2)
    picked_rows(2)

    pulled = col_next * column_products(False)
    primal_next = jnp.maximum(primal - primal_rate * (cost_hat - pulled), 0.0)
    primal_out[...] = primal_next
    bar = (2.0 * primal_next - primal).astype(BF16).astype(F32)
    row_products(high_low(col_next * (bar - 3.0 * primal)), False)
    stage_up(buf_c.at[3], row_parts)
    send_core(3)
    to_owner_direct(3, send_one, recv_last)
    rest = row_factor * own_total_direct(3, send_one, recv_last)
    dual_next = dual + dual_rate * (demand_hat - (1.5 * pushed + rest))
    dual_out[:, 0:128] = dual_next[0:4]
    dual_out[:, 128:256] = dual_next[4:8]

    wait_bytes(along_in, send_sem.at[NAMES])
    wait_bytes(names_in, send_sem.at[NAMES_CORE])
    wait_bytes(scal_x, send_sem.at[SCAL_X])
    wait_bytes(scal_in, send_sem.at[SCAL_PLANE])
    wait_bytes(buf_a.at[0, 1:4], send_sem.at[UP_X])
    wait_bytes(recv_b.at[0], send_sem.at[UP_PLANE])
    for t, into in enumerate((recv_c.at[0], recv_c.at[1], recv_c.at[2], recv_last)):
        wait_bytes(buf_c.at[t, 1], send_sem.at[UP_CORE + t])
        wait_bytes(into, send_sem.at[UP_ALL + t])
    for t in range(3):
        wait_bytes(recv_last, send_sem.at[DOWN_ALL + t])
        wait_bytes(recv_a.at[t], send_sem.at[DOWN_CORE + t])


def hand_over(primal, dual, primal_out, dual_out):
    primal_out[...] = primal[...]
    dual_out[...] = dual[...]


def on_device(tile_values, tile_rows, tile_cols, objective, demand, primal_step, dual_step):
    vmem = pl.BlockSpec(memory_space=pltpu.VMEM)
    hbm = pl.BlockSpec(memory_space=pl.ANY)
    smem = pl.BlockSpec(memory_space=pltpu.SMEM)
    shapes = (
        jax.ShapeDtypeStruct(objective.shape, F32),
        jax.ShapeDtypeStruct(demand.shape, F32),
    )
    results = pl.pallas_call(
        kernel,
        out_shape=tuple(pltpu.VMEM(shape.shape, F32) for shape in shapes),
        in_specs=[hbm, hbm, smem, smem, hbm, hbm, hbm],
        out_specs=(vmem, vmem),
        scratch_shapes=[
            pltpu.SMEM(tile_rows.shape, jnp.int32),
            pltpu.SMEM(tile_cols.shape, jnp.int32),
            pltpu.VMEM(objective.shape, F32),
            pltpu.VMEM(demand.shape, F32),
            pltpu.VMEM((TILES, 512, 256), BF16),
            pltpu.VMEM((TILES, 256, 512), BF16),
            pltpu.VMEM((24, 128), jnp.int32),
            pltpu.VMEM((24, 128), jnp.int32),
            pltpu.VMEM((1, 128), jnp.int32),
            pltpu.VMEM((3, 1, 128), jnp.int32),
            pltpu.VMEM((16, 512), F32),
            pltpu.VMEM((16, 512), F32),
            pltpu.VMEM((16, 256), F32),
            pltpu.VMEM((1, 4, 32, 512), BF16),
            pltpu.VMEM((1, 16, 8, 256), F32),
            pltpu.VMEM((1, 31, 8, 128), F32),
            pltpu.VMEM((4, 2, 32, 512), BF16),
            pltpu.VMEM((3, 2, 32, 8, 128), F32),
            pltpu.VMEM((3, 63, 8, 128), F32),
            pltpu.VMEM((2, 32, 8, 128), BF16),
            pltpu.VMEM((63, 8, 128), BF16),
            pltpu.VMEM((3, 8, 128), BF16),
            pltpu.VMEM((3, 2, 32, 8, 128), BF16),
            pltpu.VMEM((3, 2, 16, 512), BF16),
            pltpu.VMEM((3, 16, 512), BF16),
            pltpu.VMEM((16, 512), F32),
            pltpu.VMEM((128, 256), BF16),
            pltpu.VMEM((256, 128), BF16),
            pltpu.VMEM((64, 256), BF16),
            pltpu.VMEM((1, 128), F32),
            pltpu.VMEM((3, 1, 128), F32),
            pltpu.VMEM((1, 128), F32),
            pltpu.VMEM((31, 1, 128), F32),
            pltpu.VMEM((8, 128), F32),
            pltpu.SemaphoreType.DMA((TILES // LOAD,)),
            pltpu.SemaphoreType.DMA((4,)),
            pltpu.SemaphoreType.REGULAR,
            pltpu.SemaphoreType.DMA((STAGES,)),
            pltpu.SemaphoreType.DMA((STAGES,)),
        ],
        compiler_params=pltpu.CompilerParams(collective_id=0, has_side_effects=True),
    )(
        tile_rows,
        tile_cols,
        primal_step,
        dual_step,
        tile_values,
        objective,
        demand,
    )
    results = [pltpu.with_memory_space_constraint(r, pltpu.VMEM) for r in results]
    return pl.pallas_call(
        hand_over, out_shape=shapes, in_specs=[vmem, vmem], out_specs=(vmem, vmem)
    )(*results)


def solution(mesh):
    devices = mesh.devices.reshape(mesh.shape["grp"], 2, 4, 4, 2)
    return jax.shard_map(
        on_device,
        mesh=Mesh(devices, AXES),
        in_specs=(P(WIDE, None, "grp"), P(WIDE), P(WIDE), P(WIDE, "grp"), P(WIDE, "grp"), P(), P()),
        out_specs=(P(WIDE, "grp"), P(WIDE, "grp")),
        check_vma=False,
    )
```
